128 devices in a mesh: gx: 8 (over y, core), gy: 16 (over z, x).
Axes of the slice: x: 4, y: 4, z: 4, core: 2. Of those that a mesh axis runs over, the one named last changes fastest.
Arguments:
- volume_sens: float32 [3, 256, 512, 128], P(None, 'gx', 'gy'), may hold values from -6 to 6
- stiffness: float32 [256, 512, 128], P('gx', 'gy'), may hold values from 0.25 to 4
- patch_of_row: int32 [128, 1024, 1], P(('gx', 'gy')), may hold values from 0 to 127; in each aligned block of 1024 rows (0 to 1023, 1024 to 2047, ..., all dimensions but the last counted through in order) at most 32 rows name the same one
- knot_spans: int32 [128, 1024, 2], P(('gx', 'gy')), may hold values from 0 to 60
- span_params: float32 [128, 1024, 2], P(('gx', 'gy')), may hold values from 0 to 1
Outputs:
- adjoint_field: float32 [3, 256, 512, 128], P(None, 'gx', 'gy')
- control_grad: float32 [128, 3, 64, 64], P(('gx', 'gy'))
The draws below stay inside these ranges and needn't reach their ends.
Inputs may be any that keep to these rules, and one draw needn't show every extreme that they name: `patch_of_row`: the surface nodes of one device name any one patch at most 32 times; in every draw some device names some patch exactly 32 times.
All inputs are finite; a program needn't handle non-finite values.
Results may differ from the reference program's by a relative error of at most 0.000092.
Values sent between devices are 32-bit elements; how exact they have to be, the bound alone decides.
No kernel may reach another device: no remote copies, remote signals or barrier semaphores. Data moves between devices by JAX's collectives and lax.ppermute only.
A program may use at most 192 MiB of HBM per device.

```python
import math
import jax
import jax.numpy as jnp
import numpy as np

CX = 32
CY = 32
SWEEPS = 3
NC = 64
RS = 1024
CAP = 32
NX = 256
NY = 512
NZ = 128
PATCHES = 128
N_GX = 8
N_GY = 16
DEVICES = 128


def draw_stiffness(key, part):
    key_soft, key_stiff, key_linex, key_liney = jax.random.split(key, 4)
    shape = (NX, NY, NZ)
    soft = jnp.exp(jax.random.uniform(key_soft, shape, jnp.float32, math.log(0.25), math.log(0.8)))
    stiff = jnp.exp(jax.random.uniform(key_stiff, shape, jnp.float32, math.log(2.0), math.log(4.0)))
    share = 0.2
    along_x = jax.random.bernoulli(key_linex, share, (1, NY, NZ))
    along_y = jax.random.bernoulli(key_liney, share, (NX, 1, NZ))
    channel = jnp.logical_or(along_x, along_y)
    return jnp.clip(jnp.where(channel, stiff, soft), 0.25, 4.0).astype(jnp.float32)


def touch_ends(result, key, low, top_value):
    longest = result.shape.index(max(result.shape))
    spots = []
    for shift in (0, 1):
        where = [jax.random.randint(jax.random.fold_in(key, axis), (), 0, length) for axis, length in enumerate(result.shape)]
        where[longest] = (where[longest] + shift) % result.shape[longest]
        spots.append(tuple(where))
    return result.at[spots[0]].set(low).at[spots[1]].set(top_value)


def level_of(stream_key, shape, cuts, smallest, top_value):
    def one(dim, blocks):
        steps = jax.random.uniform(jax.random.fold_in(jax.random.fold_in(stream_key, 6), dim), (blocks,), jnp.float32, smallest / len(cuts), top_value / len(cuts))
        return jnp.repeat(jnp.exp(steps), shape[dim] // blocks).reshape((-1,) + (1,) * (len(shape) - dim - 1))

    gain = one(*cuts[0])
    for cut in cuts[1:]:
        gain = gain * one(*cut)
    return gain


def routed_block(stream_key, own, number, rows, number_of, top, reach, slope):
    sequence = jax.random.permutation(stream_key, number_of)
    packed, common = portions_of(number_of, rows * top, reach, slope, True), portions_of(number_of, rows * top, reach, slope, False)
    places = jnp.arange(number_of)

    def named(sizes, turn):
        used = int((sizes > 0).sum())
        fixed = max(1, used // 4)
        shifted = fixed + (places - fixed + turn * (used - fixed)) % max(1, number_of - fixed)
        return jnp.zeros((number_of,), jnp.int32).at[sequence[jnp.where(places < fixed, places, shifted)]].set(jnp.asarray(sizes, jnp.int32))

    sizes = jnp.where(number % 4 == 0, named(packed, number // 4), named(common, number - number // 4 - 1))
    mixed = jax.random.permutation(jax.random.fold_in(own, 3), number_of)
    source_of, sink = mixed[0:number_of // 2 * 2:2], mixed[1:number_of // 2 * 2:2]
    margin = jnp.minimum(sizes[source_of] - 1, reach - sizes[sink]) // 2
    margin = jnp.where((source_of == sequence[0]) | (sink == sequence[0]) | (sizes[sink] == 0), 0, jnp.maximum(margin, 0))
    shifted = jax.random.randint(jax.random.fold_in(own, 4), (number_of // 2,), 0, 1 << 20) % (margin + 1)
    sizes = sizes.at[source_of].add(-shifted).at[sink].add(shifted)
    items = jnp.searchsorted(jnp.cumsum(sizes), jnp.arange(rows * top), side="right").astype(jnp.int32)
    listing = items.reshape(top, rows).T
    listing = listing[jax.random.permutation(jax.random.fold_in(own, 1), rows)]
    turn = jax.random.randint(jax.random.fold_in(own, 2), (rows, 1), 0, top)
    return jnp.take_along_axis(listing, (jnp.arange(top)[None, :] + turn) % top, axis=1)


def portions_of(amount, total, limit, slope, full):
    portions = [(1 << 20) // math.isqrt(rank ** slope) + 1 for rank in range(1, amount + 1)]
    largest = limit if full else min(limit, max(-(-total // amount), total * portions[0] // sum(portions)))
    least = 1 if total - largest >= amount - 1 else 0
    holding, rest = [largest] + [least] * (amount - 1), total - largest - least * (amount - 1)
    while rest > 0:
        free = [i for i in range(1, amount) if holding[i] < largest] or [i for i in range(1, amount) if holding[i] < limit]
        pool, budget = sum([portions[i] for i in free]), rest
        for i in free:
            extra = min(limit - holding[i], max(1, budget * portions[i] // pool), rest)
            holding[i] = holding[i] + extra
            rest = rest - extra
    return np.array(holding)


def bell_draw(stream_key, shape, deviation, reach, cuts=(), kind=jnp.bfloat16):
    values = deviation * jax.random.normal(stream_key, shape, jnp.float32)
    if cuts:
        values = values * level_of(stream_key, shape, cuts, -0.22, 0.18)
    return jnp.clip(values, -reach, reach).astype(kind)


def setup_inputs(seed: int = 0) -> dict:
    seeds = jax.random.split(jax.random.key(seed), 6)
    volume_sens = bell_draw(seeds[0], (3, NX, NY, NZ), 1.0, 6.0, ((1, 8), (2, 16)), jnp.float32)
    stiffness = draw_stiffness(jax.random.fold_in(seeds[5], 71), 0)
    patch_of_row_keys = jax.random.split(jax.random.fold_in(seeds[2], 1), DEVICES * RS // RS)
    patch_of_row_turns = jax.random.permutation(jax.random.fold_in(seeds[2], 3), DEVICES * RS // RS)
    patch_of_row = jax.vmap(lambda own, number: routed_block(jax.random.fold_in(seeds[2], 2), own, number, RS, PATCHES, 1, CAP, 2))(patch_of_row_keys, patch_of_row_turns).reshape((DEVICES, RS, 1))
    knot_spans = touch_ends(jax.random.randint(seeds[3], (DEVICES, RS, 2), 0, NC - 3), jax.random.fold_in(seeds[3], 1), 0, (NC - 3) - 1).astype(jnp.int32)
    span_params = jnp.clip(1.0 * jax.random.uniform(seeds[4], (DEVICES, RS, 2), jnp.float32) ** level_of(seeds[4], (DEVICES, RS, 2), ((0, 128),), -0.2, 0.2), 0.0, 1.0)
    return {"volume_sens": volume_sens, "stiffness": stiffness, "patch_of_row": patch_of_row, "knot_spans": knot_spans, "span_params": span_params}


omega_relax = 2.0 / 3.0


def six_sides(padded):
    return [padded[..., 2:, 1:-1, 1:-1], padded[..., :-2, 1:-1, 1:-1],
            padded[..., 1:-1, 2:, 1:-1], padded[..., 1:-1, :-2, 1:-1],
            padded[..., 1:-1, 1:-1, 2:], padded[..., 1:-1, 1:-1, :-2]]


def pieces(param):
    other = 1.0 - param
    return [other * other * other / 6.0,
            (3.0 * param ** 3 - 6.0 * param * param + 4.0) / 6.0,
            (-3.0 * param ** 3 + 3.0 * param * param + 3.0 * param + 1.0) / 6.0,
            param ** 3 / 6.0]


def reference(volume_sens, stiffness, patch_of_row, knot_spans, span_params):
    stiff_pad = jnp.pad(stiffness, 1)
    weights = [(stiffness + side) * 0.5 for side in six_sides(stiff_pad)]
    diag = weights[0] + weights[1] + weights[2] + weights[3] + weights[4] + weights[5]
    field = volume_sens
    for sweep in range(SWEEPS):
        scaled = field / diag[None]
        scaled_pad = jnp.pad(scaled, ((0, 0), (1, 1), (1, 1), (1, 1)))
        sides = six_sides(scaled_pad)
        total = jnp.zeros_like(field)
        for index in range(6):
            total = total + weights[index][None] * sides[index]
        field = volume_sens + (1.0 - omega_relax) * field + omega_relax * total
    surface = omega_relax * field[:, :, :, 0] / diag[None, :, :, 0]
    surface = surface.reshape(3, N_GX, CX, N_GY, CY).transpose(0, 1, 3, 2, 4).reshape(3, N_GX * N_GY * RS)
    patch = patch_of_row.reshape(-1).astype(jnp.int32)
    span_a = knot_spans[:, :, 0].reshape(-1).astype(jnp.int32)
    span_e = knot_spans[:, :, 1].reshape(-1).astype(jnp.int32)
    basis_u = pieces(span_params[:, :, 0].reshape(-1))
    basis_v = pieces(span_params[:, :, 1].reshape(-1))
    grads = jnp.zeros((PATCHES, NC, NC, 3), jnp.float32)
    for first in range(4):
        for second in range(4):
            value = (basis_u[first] * basis_v[second])[None] * surface
            grads = grads.at[patch, span_a + first, span_e + second].add(value.T)
    return field, grads.transpose(0, 3, 1, 2)
```

```python
import jax
import jax.numpy as jnp
from jax import lax
from jax.experimental import pallas as pl
from jax.experimental.pallas import tpu as pltpu
from jax.sharding import PartitionSpec as P

NC = 64
OMEGA = 2.0 / 3.0
KEEP = 1.0 - OMEGA
NX = 32
NY = 32
NZ = 128
ROWS = NX * NY
CAP = 32
DEV = 128
EX = NX + 8
EY = NY + 8
SLAB_V = 36 * 9
SLAB = SLAB_V + 38 * 4 + 4
F32 = jnp.float32
BF16 = jnp.bfloat16
VMEM_LIMIT = 40 * 1024 * 1024


def vmem():
    return pl.BlockSpec(memory_space=pltpu.VMEM)


def params():
    return pltpu.CompilerParams(vmem_limit_bytes=VMEM_LIMIT)


def is_even(axis):
    return lax.rem(lax.axis_index(axis), 2) == 0


def pairings(axis):
    count = lax.axis_size(axis)
    first = [(i, i ^ 1) for i in range(count)]
    second = [(i, ((i + 1) ^ 1) - 1) for i in range(1, count - 1)]
    return first, second


def swap(axis, one, two):
    first, second = pairings(axis)
    return lax.ppermute(one, axis, first), lax.ppermute(two, axis, second)


def two_pieces(x):
    high = x.astype(BF16)
    return high, (x - high.astype(F32)).astype(BF16)


def three_pieces(x):
    high = x.astype(BF16)
    rest = x - high.astype(F32)
    mid = rest.astype(BF16)
    return high, mid, (rest - mid.astype(F32)).astype(BF16)


def dot(a, b):
    return jnp.dot(a, b, preferred_element_type=F32)


def dot_nt(a, b):
    return lax.dot_general(a, b, (((1,), (1,)), ((), ())), preferred_element_type=F32)


def x_message_kernel(vs_lo, vs_hi, c_lo, c_hi, one, two):
    def fill(low, high):
        low[0:9] = vs_lo[:, 0:3].reshape(9, NY, NZ)
        low[9:13] = c_lo[...]
        high[0:9] = vs_hi[:, 1:4].reshape(9, NY, NZ)
        high[9:13] = c_hi[...]

    even = is_even("gx")

    @pl.when(even)
    def _():
        fill(two, one)

    @pl.when(jnp.logical_not(even))
    def _():
        fill(one, two)


def x_messages(vs, c):
    shape = jax.ShapeDtypeStruct((13, NY, NZ), F32)
    return pl.pallas_call(
        x_message_kernel,
        out_shape=(shape, shape),
        grid=(1,),
        in_specs=[
            pl.BlockSpec((3, 4, NY, NZ), lambda i: (0, 0, 0, 0)),
            pl.BlockSpec((3, 4, NY, NZ), lambda i: (0, 7, 0, 0)),
            pl.BlockSpec((4, NY, NZ), lambda i: (0, 0, 0)),
            pl.BlockSpec((4, NY, NZ), lambda i: (7, 0, 0)),
        ],
        out_specs=(
            pl.BlockSpec((13, NY, NZ), lambda i: (0, 0, 0)),
            pl.BlockSpec((13, NY, NZ), lambda i: (0, 0, 0)),
        ),
        name="x_messages",
    )(vs, vs, c, c)


def y_message_kernel(vs_lo, vs_hi, c_lo, c_hi, got_one, got_two, one, two):
    even_x = is_even("gx")
    even_y = is_even("gy")

    def slab(out, vs_ref, c_ref, low, start, x_low, x_high):
        v0 = 0 if low else 5
        c0 = 0 if low else 4
        for i in range(36):
            x = i - 2
            for k in range(3):
                if x < 0:
                    piece = x_low[3 * k + 3 + x, start + v0 : start + v0 + 3]
                elif x < NX:
                    piece = vs_ref[k, x, v0 : v0 + 3]
                else:
                    piece = x_high[3 * k + x - NX, start + v0 : start + v0 + 3]
                out[9 * i + 3 * k : 9 * i + 3 * k + 3] = piece
        for i in range(38):
            x = i - 3
            if x < 0:
                piece = x_low[9 + 4 + x, start + c0 : start + c0 + 4]
            elif x < NX:
                piece = c_ref[x, c0 : c0 + 4]
            else:
                piece = x_high[9 + x - NX, start + c0 : start + c0 + 4]
            out[SLAB_V + 4 * i : SLAB_V + 4 * i + 4] = piece

    def fill(low_out, high_out, x_low, x_high):
        slab(low_out, vs_lo, c_lo, True, 0, x_low, x_high)
        slab(high_out, vs_hi, c_hi, False, 24, x_low, x_high)

    for want_x in (True, False):
        for want_y in (True, False):

            @pl.when(jnp.logical_and(even_x == want_x, even_y == want_y))
            def _():
                x_low, x_high = (got_two, got_one) if want_x else (got_one, got_two)
                low_out, high_out = (two, one) if want_y else (one, two)
                fill(low_out, high_out, x_low, x_high)


def y_messages(vs, c, got_one, got_two):
    shape = jax.ShapeDtypeStruct((SLAB, NZ), F32)
    whole = pl.BlockSpec((13, NY, NZ), lambda i: (0, 0, 0))
    return pl.pallas_call(
        y_message_kernel,
        out_shape=(shape, shape),
        grid=(1,),
        in_specs=[
            pl.BlockSpec((3, NX, 8, NZ), lambda i: (0, 0, 0, 0)),
            pl.BlockSpec((3, NX, 8, NZ), lambda i: (0, 0, 3, 0)),
            pl.BlockSpec((NX, 8, NZ), lambda i: (0, 0, 0)),
            pl.BlockSpec((NX, 8, NZ), lambda i: (0, 3, 0)),
            whole,
            whole,
        ],
        out_specs=(
            pl.BlockSpec((SLAB, NZ), lambda i: (0, 0)),
            pl.BlockSpec((SLAB, NZ), lambda i: (0, 0)),
        ),
        name="y_messages",
    )(vs, vs, c, c, got_one, got_two)


def route_kernel(patch, spans, par, to_patch, to_slot, meta):
    patch_row = patch[...]
    hot = (lax.broadcasted_iota(jnp.int32, (DEV, ROWS), 0) == patch_row).astype(F32)
    hot16 = hot.astype(BF16)
    to_patch[...] = hot16
    upper = (
        lax.broadcasted_iota(jnp.int32, (128, 128), 0)
        <= lax.broadcasted_iota(jnp.int32, (128, 128), 1)
    ).astype(BF16)
    before = jnp.zeros((DEV, 1), F32)
    ranks = []
    for block in range(ROWS // 128):
        part = slice(128 * block, 128 * block + 128)
        count = dot(hot16[:, part], upper) + before
        ranks.append(jnp.sum(count * hot[:, part], axis=0, keepdims=True) - 1.0)
        before = count[:, 127:128]
    rank = jnp.concatenate(ranks, axis=1)
    lane_slot = lax.rem(lax.broadcasted_iota(jnp.int32, (128, ROWS), 0), CAP).astype(F32)
    slot_hot = (lane_slot == rank).astype(F32)
    to_slot[...] = slot_hot.T
    fields = [
        spans[0:1].astype(F32),
        spans[1:2].astype(F32),
        par[0:1],
        par[1:2],
    ]
    spread = jnp.concatenate(
        [slot_hot[CAP * f : CAP * f + CAP] * fields[f] for f in range(4)], axis=0
    )
    high, mid, low = three_pieces(spread)
    meta[...] = dot_nt(hot16, high) + dot_nt(hot16, mid) + dot_nt(hot16, low)


def route(patch, spans, par):
    return pl.pallas_call(
        route_kernel,
        out_shape=(
            jax.ShapeDtypeStruct((DEV, ROWS), BF16),
            jax.ShapeDtypeStruct((ROWS, 128), F32),
            jax.ShapeDtypeStruct((DEV, 128), F32),
        ),
        in_specs=[vmem()] * 3,
        out_specs=(vmem(),) * 3,
        compiler_params=params(),
        cost_estimate=pl.CostEstimate(flops=400_000_000, bytes_accessed=2_000_000, transcendentals=0),
        name="route",
    )(patch, spans, par)


def up(x):
    return pltpu.roll(x, x.shape[0] - 1, 0)


def down(x):
    return pltpu.roll(x, 1, 0)


def sweep_kernel(
    vs, c, xa, xb, ya, yb, to_patch, to_slot, meta, field, send,
    stiff, ratio, wx, wy, wz, y0, y1, y2, spread,
):
    even_x = is_even("gx")
    even_y = is_even("gy")
    for k in range(3):
        y0[k, 4:36, 0:NY] = vs[k]
    stiff[4:36, 0:NY] = c[...]

    def put_x(low, high):
        for k in range(3):
            y0[k, 1:4, 0:NY] = low[3 * k : 3 * k + 3]
            y0[k, 36:39, 0:NY] = high[3 * k : 3 * k + 3]
        stiff[0:4, 0:NY] = low[9:13]
        stiff[36:40, 0:NY] = high[9:13]

    def put_y(low, high):
        for i in range(36):
            for k in range(3):
                row = 9 * i + 3 * k
                y0[k, i + 2, 32:35] = high[row : row + 3]
                y0[k, i + 2, 37:40] = low[row : row + 3]
        for i in range(38):
            row = SLAB_V + 4 * i
            stiff[i + 1, 32:36] = high[row : row + 4]
            stiff[i + 1, 36:40] = low[row : row + 4]

    @pl.when(even_x)
    def _():
        put_x(xb, xa)

    @pl.when(jnp.logical_not(even_x))
    def _():
        put_x(xa, xb)

    @pl.when(even_y)
    def _():
        put_y(yb, ya)

    @pl.when(jnp.logical_not(even_y))
    def _():
        put_y(ya, yb)

    lane = lax.broadcasted_iota(jnp.int32, (EY, NZ), 1)
    not_last = lane < NZ - 1
    not_first = lane > 0

    def prepare(x, carry):
        here = stiff[x]
        after = stiff[x + 1]
        y_next = up(here)
        z_next = jnp.where(not_last, pltpu.roll(here, NZ - 1, 1), 0.0)
        z_prev = jnp.where(not_first, pltpu.roll(here, 1, 1), 0.0)
        sides = (stiff[x - 1] + after) + (y_next + down(here)) + (z_next + z_prev)
        diag = 3.0 * here + 0.5 * sides
        inverse = jnp.where(here > 0.0, 1.0 / diag, 0.0)
        ratio[x] = OMEGA * inverse
        wx[x] = 0.5 * (here + after)
        wy[x] = 0.5 * (here + y_next)
        wz[x] = jnp.where(not_last, 0.5 * (here + z_next), 0.0)
        for k in range(3):
            y0[k, x] = y0[k, x] * inverse
        return carry

    lax.fori_loop(1, 39, prepare, 0)

    def update(source, k, x):
        here = source[k, x]
        face_y = wy[x]
        face_z = wz[x]
        total = wx[x] * source[k, x + 1] + wx[x - 1] * source[k, x - 1]
        total = total + (face_y * up(here) + down(face_y * here))
        total = total + (
            face_z * pltpu.roll(here, NZ - 1, 1) + pltpu.roll(face_z * here, 1, 1)
        )
        return y0[k, x] + KEEP * here + ratio[x] * total

    def sweep(source, target, first, last):
        def step(x, carry):
            for k in range(3):
                target[k, x] = update(source, k, x)
            return carry

        lax.fori_loop(first, last, step, 0)

    sweep(y0, y1, 2, 38)
    sweep(y1, y2, 3, 37)

    lane_field = lax.broadcasted_iota(jnp.int32, (NY, NZ), 1)

    def last_step(x, carry):
        scale = stiff[x]
        sides = (stiff[x - 1] + stiff[x + 1]) + (up(scale) + down(scale))
        z_next = jnp.where(not_last, pltpu.roll(scale, NZ - 1, 1), 0.0)
        z_prev = jnp.where(not_first, pltpu.roll(scale, 1, 1), 0.0)
        diag = (3.0 * scale + 0.5 * (sides + (z_next + z_prev)))[0:NY]
        picked = jnp.zeros((NY, NZ), F32)
        for k in range(3):
            fresh = update(y2, k, x)[0:NY]
            field[k, x - 4] = fresh * diag
            wide = jnp.broadcast_to(fresh[:, 0:1], (NY, NZ))
            picked = jnp.where(lane_field // CAP == k, wide, picked)
        rows = pl.ds(pl.multiple_of((x - 4) * NY, NY), NY)
        spread[rows] = (OMEGA * picked) * to_slot[rows]
        return carry

    lax.fori_loop(4, 36, last_step, 0)
    high, mid, low = three_pieces(spread[...])
    hot = to_patch[...]
    send[:, 0:128] = meta[...]
    send[:, 128:256] = dot(hot, high) + dot(hot, mid) + dot(hot, low)


def sweeps(vs, c, xa, xb, ya, yb, to_patch, to_slot, meta):
    plane = pltpu.VMEM((EX, EY, NZ), F32)
    cube = pltpu.VMEM((3, EX, EY, NZ), F32)
    return pl.pallas_call(
        sweep_kernel,
        out_shape=(
            jax.ShapeDtypeStruct((3, NX, NY, NZ), F32),
            jax.ShapeDtypeStruct((DEV, 256), F32),
        ),
        in_specs=[vmem()] * 9,
        out_specs=(vmem(),) * 2,
        scratch_shapes=[plane] * 5 + [cube] * 3 + [pltpu.VMEM((ROWS, 128), F32)],
        compiler_params=params(),
        cost_estimate=pl.CostEstimate(flops=60_000_000, bytes_accessed=6_000_000, transcendentals=0),
        name="sweeps",
    )(vs, c, xa, xb, ya, yb, to_patch, to_slot, meta)


def pieces(param):
    other = 1.0 - param
    return [
        other * other * other / 6.0,
        (3.0 * param * param * param - 6.0 * param * param + 4.0) / 6.0,
        (-3.0 * param * param * param + 3.0 * param * param + 3.0 * param + 1.0) / 6.0,
        param * param * param / 6.0,
    ]


def gather_kernel(got, grads, table, left, right):
    table[0:128] = got[:, 0:128].T
    table[128:256] = got[:, 128:256].T
    basis_u = pieces(table[64:96])
    basis_v = pieces(table[96:128])
    knot = lax.broadcasted_iota(jnp.int32, (NC, DEV), 0).astype(F32)

    def spline(span, basis, slot):
        offset = knot - table[span + slot : span + slot + 1]
        rows = jnp.zeros((NC, DEV), F32)
        for index in range(4):
            rows = jnp.where(offset == float(index), basis[index][slot : slot + 1], rows)
        return rows

    for slot in range(CAP):
        part = slice(DEV * slot, DEV * slot + DEV)
        along_u = spline(0, basis_u, slot)
        for k in range(3):
            value = table[128 + CAP * k + slot : 128 + CAP * k + slot + 1]
            high, low = two_pieces(along_u * value)
            left[NC * k : NC * k + NC, part] = high
            left[3 * NC + NC * k : 3 * NC + NC * k + NC, part] = low
        high, low = two_pieces(spline(CAP, basis_v, slot))
        right[0:NC, part] = high
        right[NC : 2 * NC, part] = low
    product = dot_nt(left[...], right[...])
    total = product[0 : 3 * NC, 0:NC] + (
        product[0 : 3 * NC, NC : 2 * NC] + product[3 * NC : 6 * NC, 0:NC]
    )
    grads[0] = total.reshape(3, NC, NC)


def gather(got):
    return pl.pallas_call(
        gather_kernel,
        out_shape=jax.ShapeDtypeStruct((1, 3, NC, NC), F32),
        in_specs=[vmem()],
        out_specs=vmem(),
        scratch_shapes=[
            pltpu.VMEM((256, DEV), F32),
            pltpu.VMEM((6 * NC, DEV * CAP), BF16),
            pltpu.VMEM((2 * NC, DEV * CAP), BF16),
        ],
        compiler_params=params(),
        cost_estimate=pl.CostEstimate(flops=400_000_000, bytes_accessed=200_000, transcendentals=0),
        name="gather",
    )(got)


def body(volume_sens, stiffness, patch_of_row, knot_spans, span_params):
    one, two = x_messages(volume_sens, stiffness)
    xa, xb = swap("gx", one, two)
    to_patch, to_slot, meta = route(
        patch_of_row.reshape(1, ROWS), knot_spans[0].T, span_params[0].T
    )
    one, two = y_messages(volume_sens, stiffness, xa, xb)
    ya, yb = swap("gy", one, two)
    field, send = sweeps(volume_sens, stiffness, xa, xb, ya, yb, to_patch, to_slot, meta)
    got = lax.all_to_all(send, ("gx", "gy"), 0, 0, tiled=True)
    return field, gather(got)


def solution(mesh):
    placed = (
        P(None, "gx", "gy", None),
        P("gx", "gy", None),
        P(("gx", "gy"), None, None),
        P(("gx", "gy"), None, None),
        P(("gx", "gy"), None, None),
    )
    return jax.shard_map(
        body,
        mesh=mesh,
        in_specs=placed,
        out_specs=(P(None, "gx", "gy", None), P(("gx", "gy"), None, None, None)),
        check_vma=False,
    )
```

```python
import jax
import jax.numpy as jnp
from jax import lax
from jax.experimental import pallas as pl
from jax.experimental.pallas import tpu as pltpu
from jax.sharding import PartitionSpec as P

NC = 64
OMEGA = 2.0 / 3.0
KEEP = 1.0 - OMEGA
NX = 32
NY = 32
NZ = 128
ROWS = NX * NY
CAP = 32
DEV = 128
EX = NX + 8
EY = NY + 8
SLAB_V = 36 * 9
SLAB = SLAB_V + 38 * 4 + 4
F32 = jnp.float32
BF16 = jnp.bfloat16
VMEM_LIMIT = 40 * 1024 * 1024


def vmem():
    return pl.BlockSpec(memory_space=pltpu.VMEM)


def params():
    return pltpu.CompilerParams(vmem_limit_bytes=VMEM_LIMIT)


def is_even(axis):
    return lax.rem(lax.axis_index(axis), 2) == 0


def pairings(axis):
    count = lax.axis_size(axis)
    first = [(i, i ^ 1) for i in range(count)]
    second = [(i, ((i + 1) ^ 1) - 1) for i in range(1, count - 1)]
    return first, second


def swap(axis, one, two):
    first, second = pairings(axis)
    return lax.ppermute(one, axis, first), lax.ppermute(two, axis, second)


def two_pieces(x):
    high = x.astype(BF16)
    return high, (x - high.astype(F32)).astype(BF16)


def three_pieces(x):
    high = x.astype(BF16)
    rest = x - high.astype(F32)
    mid = rest.astype(BF16)
    return high, mid, (rest - mid.astype(F32)).astype(BF16)


def dot(a, b):
    return jnp.dot(a, b, preferred_element_type=F32)


def dot_nt(a, b):
    return lax.dot_general(a, b, (((1,), (1,)), ((), ())), preferred_element_type=F32)


def x_message_kernel(vs_lo, vs_hi, c_lo, c_hi, one, two):
    even = is_even("gx")
    for i in range(13):
        if i < 9:
            k, layer = divmod(i, 3)
            low, high = vs_lo[k, layer], vs_hi[k, layer + 1]
        else:
            low, high = c_lo[i - 9], c_hi[i - 9]
        one[i] = jnp.where(even, high, low)
        two[i] = jnp.where(even, low, high)


def x_messages(vs, c):
    shape = jax.ShapeDtypeStruct((13, NY, NZ), F32)
    return pl.pallas_call(
        x_message_kernel,
        out_shape=(shape, shape),
        grid=(1,),
        in_specs=[
            pl.BlockSpec((3, 4, NY, NZ), lambda i: (0, 0, 0, 0)),
            pl.BlockSpec((3, 4, NY, NZ), lambda i: (0, 7, 0, 0)),
            pl.BlockSpec((4, NY, NZ), lambda i: (0, 0, 0)),
            pl.BlockSpec((4, NY, NZ), lambda i: (7, 0, 0)),
        ],
        out_specs=(vmem(), vmem()),
        name="x_messages",
    )(vs, vs, c, c)


def y_message_kernel(vs, c, got_one, got_two, one, two):
    even_x = is_even("gx")
    even_y = is_even("gy")

    def put(row, size, low, high):
        one[row : row + size] = jnp.where(even_y, high, low)
        two[row : row + size] = jnp.where(even_y, low, high)

    def halo(layer, before, part):
        first, second = got_one[layer, part], got_two[layer, part]
        return jnp.where(even_x == before, second, first)

    for i in range(36):
        x = i - 2
        for k in range(3):
            if x < 0:
                low, high = (halo(3 * k + 3 + x, True, p) for p in (slice(0, 3), slice(29, 32)))
            elif x < NX:
                low, high = vs[k, x, 0:3], vs[k, x, 29:32]
            else:
                low, high = (halo(3 * k + x - NX, False, p) for p in (slice(0, 3), slice(29, 32)))
            put(9 * i + 3 * k, 3, low, high)
    for i in range(38):
        x = i - 3
        if x < 0:
            low, high = (halo(13 + x, True, p) for p in (slice(0, 4), slice(28, 32)))
        elif x < NX:
            low, high = c[x, 0:4], c[x, 28:32]
        else:
            low, high = (halo(9 + x - NX, False, p) for p in (slice(0, 4), slice(28, 32)))
        put(SLAB_V + 4 * i, 4, low, high)


def y_messages(vs, c, got_one, got_two):
    shape = jax.ShapeDtypeStruct((SLAB, NZ), F32)
    return pl.pallas_call(
        y_message_kernel,
        out_shape=(shape, shape),
        in_specs=[vmem()] * 4,
        out_specs=(vmem(), vmem()),
        compiler_params=params(),
        name="y_messages",
    )(vs, c, got_one, got_two)


def route_kernel(patch, spans, par, to_patch, to_slot, meta):
    patch_row = patch[...]
    hot = (lax.broadcasted_iota(jnp.int32, (DEV, ROWS), 0) == patch_row).astype(F32)
    hot16 = hot.astype(BF16)
    to_patch[...] = hot16
    upper = (
        lax.broadcasted_iota(jnp.int32, (128, 128), 0)
        <= lax.broadcasted_iota(jnp.int32, (128, 128), 1)
    ).astype(BF16)
    before = jnp.zeros((DEV, 1), F32)
    ranks = []
    for block in range(ROWS // 128):
        part = slice(128 * block, 128 * block + 128)
        count = dot(hot16[:, part], upper) + before
        ranks.append(jnp.sum(count * hot[:, part], axis=0, keepdims=True) - 1.0)
        before = count[:, 127:128]
    rank = jnp.concatenate(ranks, axis=1)
    lane_slot = lax.rem(lax.broadcasted_iota(jnp.int32, (128, ROWS), 0), CAP).astype(F32)
    slot_hot = (lane_slot == rank).astype(F32)
    to_slot[...] = slot_hot.T
    fields = [
        spans[0:1].astype(F32),
        spans[1:2].astype(F32),
        par[0:1],
        par[1:2],
    ]
    spread = jnp.concatenate(
        [slot_hot[CAP * f : CAP * f + CAP] * fields[f] for f in range(4)], axis=0
    )
    high, mid, low = three_pieces(spread)
    meta[...] = dot_nt(hot16, high) + dot_nt(hot16, mid) + dot_nt(hot16, low)


def route(patch, spans, par):
    return pl.pallas_call(
        route_kernel,
        out_shape=(
            jax.ShapeDtypeStruct((DEV, ROWS), BF16),
            jax.ShapeDtypeStruct((ROWS, 128), F32),
            jax.ShapeDtypeStruct((DEV, 128), F32),
        ),
        in_specs=[vmem()] * 3,
        out_specs=(vmem(),) * 3,
        compiler_params=params(),
        cost_estimate=pl.CostEstimate(flops=400_000_000, bytes_accessed=2_000_000, transcendentals=0),
        name="route",
    )(patch, spans, par)


def up(x):
    return pltpu.roll(x, x.shape[0] - 1, 0)


def down(x):
    return pltpu.roll(x, 1, 0)


def sweep_kernel(
    vs, c, xa, xb, ya, yb, to_patch, to_slot, meta, field, send,
    stiff, ratio, wx, wy, wz, scale, halo, y0, y1, y2, spread, out, sem,
):
    even_x = is_even("gx")
    even_y = is_even("gy")

    def x_halo(layer, before):
        return jnp.where(even_x == before, xb[layer], xa[layer])

    def y_halo(first, size, before):
        rows = slice(first, first + size)
        return jnp.where(even_y == before, yb[rows], ya[rows])

    for x in range(EX):
        if x < 4:
            stiff[x, 0:NY] = x_halo(9 + x, True)
        elif x < 36:
            stiff[x, 0:NY] = c[x - 4]
        else:
            stiff[x, 0:NY] = x_halo(9 + x - 36, False)
        if 1 <= x < 39:
            row = SLAB_V + 4 * (x - 1)
            stiff[x, 32:36] = y_halo(row, 4, False)
            stiff[x, 36:40] = y_halo(row, 4, True)
        if 2 <= x < 38:
            for k in range(3):
                row = 9 * (x - 2) + 3 * k
                halo[k, x, 0:3] = y_halo(row, 3, False)
                halo[k, x, 5:8] = y_halo(row, 3, True)

    lane = lax.broadcasted_iota(jnp.int32, (EY, NZ), 1)
    not_last = lane < NZ - 1
    not_first = lane > 0

    for x in range(1, 39):
        here = stiff[x]
        after = stiff[x + 1]
        y_next = up(here)
        z_next = jnp.where(not_last, pltpu.roll(here, NZ - 1, 1), 0.0)
        z_prev = jnp.where(not_first, pltpu.roll(here, 1, 1), 0.0)
        sides = (stiff[x - 1] + after) + (y_next + down(here)) + (z_next + z_prev)
        diag = 3.0 * here + 0.5 * sides
        inverse = jnp.where(here > 0.0, 1.0 / diag, 0.0)
        ratio[x] = OMEGA * inverse
        wx[x] = 0.5 * (here + after)
        wy[x] = 0.5 * (here + y_next)
        wz[x] = jnp.where(not_last, 0.5 * (here + z_next), 0.0)
        if 4 <= x < 36:
            scale[x - 4] = diag[0:NY]
        for k in range(3):
            if x < 4:
                center = x_halo(3 * k + x - 1, True)
            elif x < 36:
                center = vs[k, x - 4]
            else:
                center = x_halo(3 * k + x - 36, False)
            y0[k, x, 0:NY] = center * inverse[0:NY]
            y0[k, x, NY:EY] = halo[k, x] * inverse[NY:EY]

    def update(source, k, x):
        here = source[k, x]
        face_y = wy[x]
        face_z = wz[x]
        total = wx[x] * source[k, x + 1] + wx[x - 1] * source[k, x - 1]
        total = total + (face_y * up(here) + down(face_y * here))
        total = total + (
            face_z * pltpu.roll(here, NZ - 1, 1) + pltpu.roll(face_z * here, 1, 1)
        )
        return y0[k, x] + KEEP * here + ratio[x] * total

    for x in range(2, 38):
        for k in range(3):
            y1[k, x] = update(y0, k, x)
    for x in range(3, 37):
        for k in range(3):
            y2[k, x] = update(y1, k, x)

    group = lax.broadcasted_iota(jnp.int32, (NY, NZ), 1) // CAP
    writes = []
    for x in range(4, 36):
        picked = jnp.zeros((NY, NZ), F32)
        for k in range(3):
            fresh = update(y2, k, x)[0:NY]
            out[k, x - 4] = fresh * scale[x - 4]
            wide = jnp.broadcast_to(fresh[:, 0:1], (NY, NZ))
            picked = jnp.where(group == k, wide, picked)
        rows = slice((x - 4) * NY, (x - 3) * NY)
        spread[rows] = (OMEGA * picked) * to_slot[rows]
        if x % 8 == 3:
            part = slice(x - 11, x - 3)
            write = pltpu.make_async_copy(
                out.at[:, part], field.at[:, part], sem.at[len(writes)]
            )
            write.start()
            writes.append(write)
    high, mid, low = three_pieces(spread[...])
    hot = to_patch[...]
    send[:, 0:128] = meta[...]
    send[:, 128:256] = dot(hot, high) + dot(hot, mid) + dot(hot, low)
    for write in writes:
        write.wait()


def sweeps(vs, c, xa, xb, ya, yb, to_patch, to_slot, meta):
    plane = pltpu.VMEM((EX, EY, NZ), F32)
    cube = pltpu.VMEM((3, EX, EY, NZ), F32)
    return pl.pallas_call(
        sweep_kernel,
        out_shape=(
            jax.ShapeDtypeStruct((3, NX, NY, NZ), F32),
            jax.ShapeDtypeStruct((DEV, 256), F32),
        ),
        in_specs=[vmem()] * 9,
        out_specs=(pl.BlockSpec(memory_space=pl.ANY), vmem()),
        scratch_shapes=[plane] * 5
        + [pltpu.VMEM((NX, NY, NZ), F32), pltpu.VMEM((3, EX, 8, NZ), F32)]
        + [cube] * 3
        + [
            pltpu.VMEM((ROWS, 128), F32),
            pltpu.VMEM((3, NX, NY, NZ), F32),
            pltpu.SemaphoreType.DMA((4,)),
        ],
        compiler_params=params(),
        cost_estimate=pl.CostEstimate(flops=60_000_000, bytes_accessed=6_000_000, transcendentals=0),
        name="sweeps",
    )(vs, c, xa, xb, ya, yb, to_patch, to_slot, meta)


def pieces(param):
    other = 1.0 - param
    return [
        other * other * other / 6.0,
        (3.0 * param * param * param - 6.0 * param * param + 4.0) / 6.0,
        (-3.0 * param * param * param + 3.0 * param * param + 3.0 * param + 1.0) / 6.0,
        param * param * param / 6.0,
    ]


def gather_kernel(got, grads, table, left, right):
    table[0:128] = got[:, 0:128].T
    table[128:256] = got[:, 128:256].T
    basis_u = pieces(table[64:96])
    basis_v = pieces(table[96:128])
    knot = lax.broadcasted_iota(jnp.int32, (NC, DEV), 0).astype(F32)

    def spline(span, basis, slot):
        offset = knot - table[span + slot : span + slot + 1]
        rows = jnp.zeros((NC, DEV), F32)
        for index in range(4):
            rows = jnp.where(offset == float(index), basis[index][slot : slot + 1], rows)
        return rows

    for slot in range(CAP):
        part = slice(DEV * slot, DEV * slot + DEV)
        along_u = spline(0, basis_u, slot)
        for k in range(3):
            value = table[128 + CAP * k + slot : 128 + CAP * k + slot + 1]
            high, low = two_pieces(along_u * value)
            left[NC * k : NC * k + NC, part] = high
            left[3 * NC + NC * k : 3 * NC + NC * k + NC, part] = low
        high, low = two_pieces(spline(CAP, basis_v, slot))
        right[0:NC, part] = high
        right[NC : 2 * NC, part] = low
    product = dot_nt(left[...], right[...])
    total = product[0 : 3 * NC, 0:NC] + (
        product[0 : 3 * NC, NC : 2 * NC] + product[3 * NC : 6 * NC, 0:NC]
    )
    grads[0] = total.reshape(3, NC, NC)


def gather(got):
    return pl.pallas_call(
        gather_kernel,
        out_shape=jax.ShapeDtypeStruct((1, 3, NC, NC), F32),
        in_specs=[vmem()],
        out_specs=vmem(),
        scratch_shapes=[
            pltpu.VMEM((256, DEV), F32),
            pltpu.VMEM((6 * NC, DEV * CAP), BF16),
            pltpu.VMEM((2 * NC, DEV * CAP), BF16),
        ],
        compiler_params=params(),
        cost_estimate=pl.CostEstimate(flops=400_000_000, bytes_accessed=200_000, transcendentals=0),
        name="gather",
    )(got)


def body(volume_sens, stiffness, patch_of_row, knot_spans, span_params):
    one, two = x_messages(volume_sens, stiffness)
    xa, xb = swap("gx", one, two)
    to_patch, to_slot, meta = route(
        patch_of_row.reshape(1, ROWS), knot_spans[0].T, span_params[0].T
    )
    one, two = y_messages(volume_sens, stiffness, xa, xb)
    ya, yb = swap("gy", one, two)
    field, send = sweeps(volume_sens, stiffness, xa, xb, ya, yb, to_patch, to_slot, meta)
    got = lax.all_to_all(send, ("gx", "gy"), 0, 0, tiled=True)
    return field, gather(got)


def solution(mesh):
    placed = (
        P(None, "gx", "gy", None),
        P("gx", "gy", None),
        P(("gx", "gy"), None, None),
        P(("gx", "gy"), None, None),
        P(("gx", "gy"), None, None),
    )
    return jax.shard_map(
        body,
        mesh=mesh,
        in_specs=placed,
        out_specs=(P(None, "gx", "gy", None), P(("gx", "gy"), None, None, None)),
        check_vma=False,
    )
```

```python
import jax
import jax.numpy as jnp
from jax import lax
from jax.experimental import pallas as pl
from jax.experimental.pallas import tpu as pltpu
from jax.sharding import PartitionSpec as P

NC = 64
OMEGA = 2.0 / 3.0
KEEP = 1.0 - OMEGA
NX = 32
NY = 32
NZ = 128
ROWS = NX * NY
CAP = 32
DEV = 128
CHUNK = 8
EX = NX + 8
EY = NY + 8
SLAB_V = 9 * NX
SLAB = 13 * NX
F32 = jnp.float32
BF16 = jnp.bfloat16
VMEM_LIMIT = 24 * 1024 * 1024


def vmem():
    return pl.BlockSpec(memory_space=pltpu.VMEM)


def params():
    return pltpu.CompilerParams(vmem_limit_bytes=VMEM_LIMIT)


def is_even(axis):
    return lax.rem(lax.axis_index(axis), 2) == 0


def exchange(along_x, one, two):
    count_x, count_y = lax.axis_size("gx"), lax.axis_size("gy")

    def partner(i, last):
        return i if i in (0, last) else ((i + 1) ^ 1) - 1

    first, second = [], []
    for i in range(count_x):
        for j in range(count_y):
            if along_x:
                near, far = (i ^ 1, j), (partner(i, count_x - 1), j)
                far = (i, j ^ 1) if far == (i, j) else far
            else:
                near, far = (i, j ^ 1), (i, partner(j, count_y - 1))
                far = (i ^ 1, j) if far == (i, j) else far
            here = i * count_y + j
            first.append((here, near[0] * count_y + near[1]))
            second.append((here, far[0] * count_y + far[1]))
    both = ("gx", "gy")
    return lax.ppermute(one, both, first), lax.ppermute(two, both, second)


def at_end(axis):
    here = lax.axis_index(axis)
    return jnp.logical_or(here == 0, here == lax.axis_size(axis) - 1)


def two_pieces(x):
    high = x.astype(BF16)
    return high, (x - high.astype(F32)).astype(BF16)


def three_pieces(x):
    high = x.astype(BF16)
    rest = x - high.astype(F32)
    mid = rest.astype(BF16)
    return high, mid, (rest - mid.astype(F32)).astype(BF16)


def dot(a, b):
    return jnp.dot(a, b, preferred_element_type=F32)


def dot_nt(a, b):
    return lax.dot_general(a, b, (((1,), (1,)), ((), ())), preferred_element_type=F32)


def message_kernel(vs, c, y_one, y_two, x_one, x_two, low_v, high_v, low_c, high_c, sems):
    slabs = [
        pltpu.make_async_copy(vs.at[:, :, 0:8], low_v, sems.at[0]),
        pltpu.make_async_copy(vs.at[:, :, NY - 8 : NY], high_v, sems.at[1]),
        pltpu.make_async_copy(c.at[:, 0:8], low_c, sems.at[2]),
        pltpu.make_async_copy(c.at[:, NY - 8 : NY], high_c, sems.at[3]),
    ]
    for copy in slabs:
        copy.start()

    def layers(low, high):
        copies = []
        for k in range(3):
            spot = slice(3 * k, 3 * k + 3)
            copies.append(pltpu.make_async_copy(vs.at[k, 0:3], low.at[spot], sems.at[4 + k]))
            copies.append(
                pltpu.make_async_copy(vs.at[k, NX - 3 : NX], high.at[spot], sems.at[7 + k])
            )
        copies.append(pltpu.make_async_copy(c.at[0:4], low.at[9:13], sems.at[10]))
        copies.append(pltpu.make_async_copy(c.at[NX - 4 : NX], high.at[9:13], sems.at[11]))
        return copies

    even_x = is_even("gx")
    even_y = is_even("gy")

    @pl.when(even_x)
    def _():
        for copy in layers(x_two, x_one):
            copy.start()

    @pl.when(jnp.logical_not(even_x))
    def _():
        for copy in layers(x_one, x_two):
            copy.start()

    inside_y = jnp.where(at_end("gy"), 0.0, 1.0)

    def put(row, size, low, high):
        y_one[row : row + size] = jnp.where(even_y, high, low)
        y_two[row : row + size] = jnp.where(even_y, low, high) * inside_y

    for copy in slabs:
        copy.wait()
    for x in range(NX):
        for k in range(3):
            put(9 * x + 3 * k, 3, low_v[k, x, 0:3], high_v[k, x, 5:8])
        put(SLAB_V + 4 * x, 4, low_c[x, 0:4], high_c[x, 4:8])

    @pl.when(even_x)
    def _():
        for copy in layers(x_two, x_one):
            copy.wait()

    @pl.when(jnp.logical_not(even_x))
    def _():
        for copy in layers(x_one, x_two):
            copy.wait()

    @pl.when(at_end("gx"))
    def _():
        x_two[...] = jnp.zeros((13, NY, NZ), F32)


def messages(vs, c):
    y_shape = jax.ShapeDtypeStruct((SLAB, NZ), F32)
    x_shape = jax.ShapeDtypeStruct((13, NY, NZ), F32)
    return pl.pallas_call(
        message_kernel,
        out_shape=(y_shape, y_shape, x_shape, x_shape),
        in_specs=[pl.BlockSpec(memory_space=pltpu.HBM)] * 2,
        out_specs=(vmem(),) * 4,
        scratch_shapes=[
            pltpu.VMEM((3, NX, 8, NZ), F32),
            pltpu.VMEM((3, NX, 8, NZ), F32),
            pltpu.VMEM((NX, 8, NZ), F32),
            pltpu.VMEM((NX, 8, NZ), F32),
            pltpu.SemaphoreType.DMA((12,)),
        ],
        compiler_params=params(),
        name="messages",
    )(vs, c)


def y_halo(even, one, two, first, size, before):
    rows = slice(first, first + size)
    return jnp.where(even == before, two[rows], one[rows])


def corner_kernel(ya, yb, _, one, two):
    even_x = is_even("gx")
    even_y = is_even("gy")
    inside_x = jnp.where(at_end("gx"), 0.0, 1.0)
    blank = jnp.zeros((2, NZ), F32)
    for i in range(13):
        if i < 9:
            k, layer = divmod(i, 3)
            size, places = 3, (9 * layer + 3 * k, 9 * (NX - 3 + layer) + 3 * k)
            one[i, 3:5] = blank
            two[i, 3:5] = blank
        else:
            size, places = 4, (SLAB_V + 4 * (i - 9), SLAB_V + 4 * (NX - 4 + i - 9))
        for spot, before in ((slice(0, size), False), (slice(8 - size, 8), True)):
            low, high = (y_halo(even_y, ya, yb, row, size, before) for row in places)
            one[i, spot] = jnp.where(even_x, high, low)
            two[i, spot] = jnp.where(even_x, low, high) * inside_x


def corners(ya, yb, meta):
    shape = jax.ShapeDtypeStruct((13, 8, NZ), F32)
    return pl.pallas_call(
        corner_kernel,
        out_shape=(shape, shape),
        in_specs=[vmem()] * 3,
        out_specs=(vmem(), vmem()),
        compiler_params=params(),
        name="corners",
    )(ya, yb, meta)


def route_kernel(patch, spans, par, to_patch, to_slot, meta):
    patch_row = patch[...]
    hot = (lax.broadcasted_iota(jnp.int32, (DEV, ROWS), 0) == patch_row).astype(F32)
    hot16 = hot.astype(BF16)
    to_patch[...] = hot16
    upper = (
        lax.broadcasted_iota(jnp.int32, (128, 128), 0)
        <= lax.broadcasted_iota(jnp.int32, (128, 128), 1)
    ).astype(BF16)
    before = jnp.zeros((DEV, 1), F32)
    ranks = []
    for block in range(ROWS // 128):
        part = slice(128 * block, 128 * block + 128)
        count = dot(hot16[:, part], upper) + before
        ranks.append(jnp.sum(count * hot[:, part], axis=0, keepdims=True) - 1.0)
        before = count[:, 127:128]
    rank = jnp.concatenate(ranks, axis=1)
    lane_slot = lax.rem(lax.broadcasted_iota(jnp.int32, (128, ROWS), 0), CAP).astype(F32)
    slot_hot = (lane_slot == rank).astype(F32)
    to_slot[...] = slot_hot.T
    fields = [
        spans[0:1].astype(F32),
        spans[1:2].astype(F32),
        par[0:1],
        par[1:2],
    ]
    spread = jnp.concatenate(
        [slot_hot[CAP * f : CAP * f + CAP] * fields[f] for f in range(4)], axis=0
    )
    high, mid, low = three_pieces(spread)
    meta[...] = dot_nt(hot16, high) + dot_nt(hot16, mid) + dot_nt(hot16, low)


def route(patch, spans, par):
    return pl.pallas_call(
        route_kernel,
        out_shape=(
            jax.ShapeDtypeStruct((DEV, ROWS), BF16),
            jax.ShapeDtypeStruct((ROWS, 128), F32),
            jax.ShapeDtypeStruct((DEV, 128), F32),
        ),
        in_specs=[vmem()] * 3,
        out_specs=(vmem(),) * 3,
        compiler_params=params(),
        cost_estimate=pl.CostEstimate(flops=400_000_000, bytes_accessed=2_000_000, transcendentals=0),
        name="route",
    )(patch, spans, par)


def up(x):
    return pltpu.roll(x, x.shape[0] - 1, 0)


def down(x):
    return pltpu.roll(x, 1, 0)


class Rows:
    def __init__(self):
        self.place = {}

    def hold(self, ref, rows):
        for index, x in enumerate(rows):
            self.place[x] = (ref, index)
        return self

    def __getitem__(self, x):
        ref, index = self.place[x]
        return ref[index]

    def __setitem__(self, x, value):
        ref, index = self.place[x]
        ref[index] = value


EDGE = [4, 5, 6, 7, 8, 31, 32, 33, 34, 35]
MIDDLE = list(range(9, 31))


class Stencil:
    def __init__(self, stiff, ratio, wx, wy, wz, scale, y0, y1, y2):
        self.stiff, self.ratio, self.scale = stiff, ratio, scale
        self.wx, self.wy, self.wz = wx, wy, wz
        self.fields = (y0, y1, y2)
        lane = lax.broadcasted_iota(jnp.int32, (EY, NZ), 1)
        self.not_last = lane < NZ - 1
        self.not_first = lane > 0
        self.group = lax.broadcasted_iota(jnp.int32, (NY, NZ), 1) // CAP

    def prepare(self, x, source):
        here, after, before = self.stiff[x], self.stiff[x + 1], self.stiff[x - 1]
        y_next = up(here)
        z_next = jnp.where(self.not_last, pltpu.roll(here, NZ - 1, 1), 0.0)
        z_prev = jnp.where(self.not_first, pltpu.roll(here, 1, 1), 0.0)
        sides = (before + after) + (y_next + down(here)) + (z_next + z_prev)
        diag = 3.0 * here + 0.5 * sides
        inverse = jnp.where(here > 0.0, 1.0 / diag, 0.0)
        self.ratio[x] = OMEGA * inverse
        self.wx[x] = 0.5 * (here + after)
        self.wy[x] = 0.5 * (here + y_next)
        self.wz[x] = jnp.where(self.not_last, 0.5 * (here + z_next), 0.0)
        self.scale[x] = diag
        for k in range(3):
            self.fields[0][k][x] = source(k, x) * inverse

    def update(self, level, k, x):
        source = self.fields[level][k]
        here = source[x]
        face_y, face_z = self.wy[x], self.wz[x]
        total = self.wx[x] * source[x + 1] + self.wx[x - 1] * source[x - 1]
        total = total + (face_y * up(here) + down(face_y * here))
        total = total + (
            face_z * pltpu.roll(here, NZ - 1, 1) + pltpu.roll(face_z * here, 1, 1)
        )
        return self.fields[0][k][x] + KEEP * here + self.ratio[x] * total

    def sweep(self, level, rows):
        for x in rows:
            for k in range(3):
                self.fields[level + 1][k][x] = self.update(level, k, x)

    def finish(self, x, out, index, slots):
        picked = jnp.zeros((NY, NZ), F32)
        for k in range(3):
            fresh = self.update(2, k, x)[0:NY]
            out[k, index] = fresh * self.scale[x][0:NY]
            wide = jnp.broadcast_to(fresh[:, 0:1], (NY, NZ))
            picked = jnp.where(self.group == k, wide, picked)
        return (OMEGA * picked) * slots


def scatter_rows(hot, spread):
    high, mid, low = three_pieces(spread)
    return dot(hot, high) + dot(hot, mid) + dot(hot, low)


def cube_rows(refs, rows):
    return [Rows().hold(ref, rows) for ref in refs]


def interior_kernel(
    vs, c, ya, yb, to_patch, to_slot, field, partial, keep, keep3,
    stiff, mids, mids3, spread, out, sem,
):
    even_y = is_even("gy")
    for x in range(NX):
        row = SLAB_V + 4 * x
        stiff[x, 0:NY] = c[x]
        stiff[x, NY : NY + 4] = y_halo(even_y, ya, yb, row, 4, False)
        stiff[x, EY - 4 : EY] = y_halo(even_y, ya, yb, row, 4, True)
    for x in range(1, NX - 1):
        for k in range(3):
            row = 9 * x + 3 * k
            place = (keep3.at[0, k], EDGE.index(x + 4)) if x + 4 in EDGE else (mids3.at[0, k], x - 5)
            ref, index = place
            ref[index, NY : NY + 3] = y_halo(even_y, ya, yb, row, 3, False)
            ref[index, EY - 3 : EY] = y_halo(even_y, ya, yb, row, 3, True)

    def source(k, x):
        ref, index = fields[0][k].place[x]
        return jnp.concatenate([vs[k, x - 4], ref[index, NY:EY]], axis=0)

    def plane(n):
        return Rows().hold(keep.at[n], EDGE).hold(mids.at[n], MIDDLE)

    fields = [
        [Rows().hold(keep3.at[n, k], EDGE).hold(mids3.at[n, k], MIDDLE) for k in range(3)]
        for n in range(3)
    ]
    grid = Stencil(
        Rows().hold(stiff, range(4, 36)), plane(0), plane(1), plane(2), plane(3), plane(4), *fields
    )
    for x in (4, 5, 34, 35):
        keep[5, EDGE.index(x)] = grid.stiff[x]
    for x in range(5, 35):
        grid.prepare(x, source)
    grid.sweep(0, range(6, 34))
    grid.sweep(1, range(7, 33))
    writes = []
    total = jnp.zeros((DEV, 128), F32)
    for x in range(8, 32):
        rows = slice((x - 4) * NY, (x - 3) * NY)
        spread[(x - 8) * NY : (x - 7) * NY] = grid.finish(x, out, x - 8, to_slot[rows])
        if x % 8 == 7:
            part = slice(x - 15, x - 7)
            last = (x - 7) * NY
            total = total + scatter_rows(
                to_patch[:, last - 128 : last + 128], spread[last - 256 : last]
            )
            write = pltpu.make_async_copy(
                out.at[:, part], field.at[:, x - 11 : x - 3], sem.at[len(writes)]
            )
            write.start()
            writes.append(write)
    partial[...] = total
    for write in writes:
        write.wait()


def interior(vs, c, ya, yb, to_patch, to_slot):
    return pl.pallas_call(
        interior_kernel,
        out_shape=(
            jax.ShapeDtypeStruct((3, NX, NY, NZ), F32),
            jax.ShapeDtypeStruct((DEV, 128), F32),
            jax.ShapeDtypeStruct((6, len(EDGE), EY, NZ), F32),
            jax.ShapeDtypeStruct((3, 3, len(EDGE), EY, NZ), F32),
        ),
        in_specs=[vmem()] * 6,
        out_specs=(pl.BlockSpec(memory_space=pl.ANY), vmem(), vmem(), vmem()),
        scratch_shapes=[
            pltpu.VMEM((NX, EY, NZ), F32),
            pltpu.VMEM((5, len(MIDDLE), EY, NZ), F32),
            pltpu.VMEM((3, 3, len(MIDDLE), EY, NZ), F32),
            pltpu.VMEM((768, 128), F32),
            pltpu.VMEM((3, 24, NY, NZ), F32),
            pltpu.SemaphoreType.DMA((3,)),
        ],
        compiler_params=params(),
        cost_estimate=pl.CostEstimate(flops=60_000_000, bytes_accessed=6_000_000, transcendentals=0),
        name="interior",
    )(vs, c, ya, yb, to_patch, to_slot)


def edge_kernel(
    vs, ya, yb, xa, xb, za, zb, to_patch, to_slot, meta, partial, keep, keep3, _, field, send,
    fresh, fresh3, spread, out, sem,
):
    even_x = is_even("gx")
    even_y = is_even("gy")

    def x_halo(layer, before):
        center = jnp.where(even_x == before, xb[layer], xa[layer])
        corner = jnp.where(even_x == before, zb[layer], za[layer])
        return jnp.concatenate([center, corner], axis=0)

    class Given:
        def __getitem__(self, x):
            if x < 4:
                return x_halo(9 + x, True)
            if x < 36:
                return keep[5, EDGE.index(x)]
            return x_halo(9 + x - 36, False)

    def source(k, x):
        if x == 4 or x == 35:
            spot = 0 if x == 4 else 1
            row = 9 * (x - 4) + 3 * k
            fresh3[3, k, spot, NY : NY + 3] = y_halo(even_y, ya, yb, row, 3, False)
            fresh3[3, k, spot, EY - 3 : EY] = y_halo(even_y, ya, yb, row, 3, True)
            return jnp.concatenate([vs[k, x - 4], fresh3[3, k, spot, NY:EY]], axis=0)
        if x < 4:
            return x_halo(3 * k + x - 1, True)
        return x_halo(3 * k + x - 36, False)

    def hold(ref3, n, k, rows):
        return Rows().hold(keep3.at[n, k], EDGE).hold(ref3.at[n, k], rows)

    first = [1, 2, 3, 4, 35, 36, 37, 38]
    second = [2, 3, 4, 5, 34, 35, 36, 37]
    third = [3, 4, 5, 6, 33, 34, 35, 36]
    last = [4, 5, 6, 7, 32, 33, 34, 35]
    planes = [Rows().hold(keep.at[n], EDGE).hold(fresh.at[n], first) for n in range(5)]
    fields = [
        [hold(fresh3, n, k, rows) for k in range(3)] for n, rows in enumerate((first, second, third))
    ]
    grid = Stencil(Given(), *planes, *fields)
    for x in first:
        grid.prepare(x, source)
    grid.sweep(0, second)
    grid.sweep(1, third)
    for index, x in enumerate(last):
        rows = slice((x - 4) * NY, (x - 3) * NY)
        spread[index * NY : (index + 1) * NY] = grid.finish(x, out, index, to_slot[rows])
    writes = [
        pltpu.make_async_copy(out.at[:, 0:4], field.at[:, 0:4], sem.at[0]),
        pltpu.make_async_copy(out.at[:, 4:8], field.at[:, 28:32], sem.at[1]),
    ]
    for write in writes:
        write.start()
    send[:, 0:128] = meta[...]
    send[:, 128:256] = (
        partial[...]
        + scatter_rows(
            jnp.concatenate([to_patch[:, 0:128], to_patch[:, 896:1024]], axis=1), spread[...]
        )
    )
    for write in writes:
        write.wait()


def edges(vs, ya, yb, xa, xb, za, zb, to_patch, to_slot, meta, partial, keep, keep3, field):
    return pl.pallas_call(
        edge_kernel,
        out_shape=(
            jax.ShapeDtypeStruct((3, NX, NY, NZ), F32),
            jax.ShapeDtypeStruct((DEV, 256), F32),
        ),
        in_specs=[vmem()] * 13 + [pl.BlockSpec(memory_space=pl.ANY)],
        out_specs=(pl.BlockSpec(memory_space=pl.ANY), vmem()),
        scratch_shapes=[
            pltpu.VMEM((5, 8, EY, NZ), F32),
            pltpu.VMEM((4, 3, 8, EY, NZ), F32),
            pltpu.VMEM((256, 128), F32),
            pltpu.VMEM((3, 8, NY, NZ), F32),
            pltpu.SemaphoreType.DMA((2,)),
        ],
        input_output_aliases={13: 0},
        compiler_params=params(),
        cost_estimate=pl.CostEstimate(flops=20_000_000, bytes_accessed=2_000_000, transcendentals=0),
        name="edges",
    )(vs, ya, yb, xa, xb, za, zb, to_patch, to_slot, meta, partial, keep, keep3, field)


def pieces(param):
    other = 1.0 - param
    return [
        other * other * other / 6.0,
        (3.0 * param * param * param - 6.0 * param * param + 4.0) / 6.0,
        (-3.0 * param * param * param + 3.0 * param * param + 3.0 * param + 1.0) / 6.0,
        param * param * param / 6.0,
    ]


def gather_kernel(got, grads, table, left, right):
    table[0:128] = got[:, 0:128].T
    table[128:256] = got[:, 128:256].T
    basis_u = pieces(table[64:96])
    basis_v = pieces(table[96:128])
    knot = lax.broadcasted_iota(jnp.int32, (NC, DEV), 0).astype(F32)

    def spline(span, basis, slot):
        offset = knot - table[span + slot : span + slot + 1]
        rows = jnp.zeros((NC, DEV), F32)
        for index in range(4):
            rows = jnp.where(offset == float(index), basis[index][slot : slot + 1], rows)
        return rows

    product = jnp.zeros((6 * NC, 2 * NC), F32)
    for slot in range(CAP):
        part = slice(DEV * slot, DEV * slot + DEV)
        along_u = spline(0, basis_u, slot)
        for k in range(3):
            value = table[128 + CAP * k + slot : 128 + CAP * k + slot + 1]
            high, low = two_pieces(along_u * value)
            left[NC * k : NC * k + NC, part] = high
            left[3 * NC + NC * k : 3 * NC + NC * k + NC, part] = low
        high, low = two_pieces(spline(CAP, basis_v, slot))
        right[0:NC, part] = high
        right[NC : 2 * NC, part] = low
        if slot % CHUNK == CHUNK - 1:
            block = slice(DEV * (slot + 1 - CHUNK), DEV * (slot + 1))
            product = product + dot_nt(left[:, block], right[:, block])
    total = product[0 : 3 * NC, 0:NC] + (
        product[0 : 3 * NC, NC : 2 * NC] + product[3 * NC : 6 * NC, 0:NC]
    )
    grads[0] = total.reshape(3, NC, NC)


def gather(got):
    return pl.pallas_call(
        gather_kernel,
        out_shape=jax.ShapeDtypeStruct((1, 3, NC, NC), F32),
        in_specs=[vmem()],
        out_specs=vmem(),
        scratch_shapes=[
            pltpu.VMEM((256, DEV), F32),
            pltpu.VMEM((6 * NC, DEV * CAP), BF16),
            pltpu.VMEM((2 * NC, DEV * CAP), BF16),
        ],
        compiler_params=params(),
        cost_estimate=pl.CostEstimate(flops=400_000_000, bytes_accessed=200_000, transcendentals=0),
        name="gather",
    )(got)


def body(volume_sens, stiffness, patch_of_row, knot_spans, span_params):
    y_one, y_two, x_one, x_two = messages(
        pltpu.with_memory_space_constraint(volume_sens, pltpu.HBM),
        pltpu.with_memory_space_constraint(stiffness, pltpu.HBM),
    )
    ya, yb = exchange(False, y_one, y_two)
    xa, xb = exchange(True, x_one, x_two)
    to_patch, to_slot, meta = route(
        patch_of_row.reshape(1, ROWS), knot_spans[0].T, span_params[0].T
    )
    za, zb = exchange(True, *corners(ya, yb, meta))
    field, partial, keep, keep3 = interior(volume_sens, stiffness, ya, yb, to_patch, to_slot)
    field, send = edges(
        volume_sens, ya, yb, xa, xb, za, zb, to_patch, to_slot, meta, partial, keep, keep3, field
    )
    got = lax.all_to_all(send, ("gx", "gy"), 0, 0, tiled=True)
    return field, gather(got)


def solution(mesh):
    placed = (
        P(None, "gx", "gy", None),
        P("gx", "gy", None),
        P(("gx", "gy"), None, None),
        P(("gx", "gy"), None, None),
        P(("gx", "gy"), None, None),
    )
    return jax.shard_map(
        body,
        mesh=mesh,
        in_specs=placed,
        out_specs=(P(None, "gx", "gy", None), P(("gx", "gy"), None, None, None)),
        check_vma=False,
    )
```

```python
import jax
import jax.numpy as jnp
from jax import lax
from jax.experimental import pallas as pl
from jax.experimental.pallas import tpu as pltpu
from jax.sharding import PartitionSpec as P

NC = 64
OMEGA = 2.0 / 3.0
KEEP = 1.0 - OMEGA
NX = 32
NY = 32
NZ = 128
ROWS = NX * NY
CAP = 32
DEV = 128
CHUNK = 8
EX = NX + 8
EY = NY + 8
SLAB_V = 9 * NX
SLAB = 13 * NX
F32 = jnp.float32
BF16 = jnp.bfloat16
VMEM_LIMIT = 24 * 1024 * 1024


def vmem():
    return pl.BlockSpec(memory_space=pltpu.VMEM)


def params():
    return pltpu.CompilerParams(vmem_limit_bytes=VMEM_LIMIT)


def is_even(axis):
    return lax.rem(lax.axis_index(axis), 2) == 0


def exchange(along_x, one, two):
    count_x, count_y = lax.axis_size("gx"), lax.axis_size("gy")

    def partner(i, last):
        return i if i in (0, last) else ((i + 1) ^ 1) - 1

    first, second = [], []
    for i in range(count_x):
        for j in range(count_y):
            if along_x:
                near, far = (i ^ 1, j), (partner(i, count_x - 1), j)
                far = (i, j ^ 1) if far == (i, j) else far
            else:
                near, far = (i, j ^ 1), (i, partner(j, count_y - 1))
                far = (i ^ 1, j) if far == (i, j) else far
            here = i * count_y + j
            first.append((here, near[0] * count_y + near[1]))
            second.append((here, far[0] * count_y + far[1]))
    both = ("gx", "gy")
    return lax.ppermute(one, both, first), lax.ppermute(two, both, second)


def at_end(axis):
    here = lax.axis_index(axis)
    return jnp.logical_or(here == 0, here == lax.axis_size(axis) - 1)


def two_pieces(x):
    high = x.astype(BF16)
    return high, (x - high.astype(F32)).astype(BF16)


def three_pieces(x):
    high = x.astype(BF16)
    rest = x - high.astype(F32)
    mid = rest.astype(BF16)
    return high, mid, (rest - mid.astype(F32)).astype(BF16)


def dot(a, b):
    return jnp.dot(a, b, preferred_element_type=F32)


def dot_nt(a, b):
    return lax.dot_general(a, b, (((1,), (1,)), ((), ())), preferred_element_type=F32)


def message_kernel(vs, c, y_one, y_two, x_one, x_two, low_v, high_v, low_c, high_c, sems):
    slabs = [
        pltpu.make_async_copy(vs.at[:, :, 0:8], low_v, sems.at[0]),
        pltpu.make_async_copy(vs.at[:, :, NY - 8 : NY], high_v, sems.at[1]),
        pltpu.make_async_copy(c.at[:, 0:8], low_c, sems.at[2]),
        pltpu.make_async_copy(c.at[:, NY - 8 : NY], high_c, sems.at[3]),
    ]
    for copy in slabs:
        copy.start()

    def layers(low, high):
        copies = []
        for k in range(3):
            spot = slice(3 * k, 3 * k + 3)
            copies.append(pltpu.make_async_copy(vs.at[k, 0:3], low.at[spot], sems.at[4 + k]))
            copies.append(
                pltpu.make_async_copy(vs.at[k, NX - 3 : NX], high.at[spot], sems.at[7 + k])
            )
        copies.append(pltpu.make_async_copy(c.at[0:4], low.at[9:13], sems.at[10]))
        copies.append(pltpu.make_async_copy(c.at[NX - 4 : NX], high.at[9:13], sems.at[11]))
        return copies

    even_x = is_even("gx")
    even_y = is_even("gy")

    @pl.when(even_x)
    def _():
        for copy in layers(x_two, x_one):
            copy.start()

    @pl.when(jnp.logical_not(even_x))
    def _():
        for copy in layers(x_one, x_two):
            copy.start()

    inside_y = jnp.where(at_end("gy"), 0.0, 1.0)

    def put(row, size, low, high):
        y_one[row : row + size] = jnp.where(even_y, high, low)
        y_two[row : row + size] = jnp.where(even_y, low, high) * inside_y

    for copy in slabs:
        copy.wait()
    for x in range(NX):
        for k in range(3):
            put(9 * x + 3 * k, 3, low_v[k, x, 0:3], high_v[k, x, 5:8])
        put(SLAB_V + 4 * x, 4, low_c[x, 0:4], high_c[x, 4:8])

    @pl.when(even_x)
    def _():
        for copy in layers(x_two, x_one):
            copy.wait()

    @pl.when(jnp.logical_not(even_x))
    def _():
        for copy in layers(x_one, x_two):
            copy.wait()

    @pl.when(at_end("gx"))
    def _():
        x_two[...] = jnp.zeros((13, NY, NZ), F32)


def messages(vs, c):
    y_shape = jax.ShapeDtypeStruct((SLAB, NZ), F32)
    x_shape = jax.ShapeDtypeStruct((13, NY, NZ), F32)
    return pl.pallas_call(
        message_kernel,
        out_shape=(y_shape, y_shape, x_shape, x_shape),
        in_specs=[pl.BlockSpec(memory_space=pltpu.HBM)] * 2,
        out_specs=(vmem(),) * 4,
        scratch_shapes=[
            pltpu.VMEM((3, NX, 8, NZ), F32),
            pltpu.VMEM((3, NX, 8, NZ), F32),
            pltpu.VMEM((NX, 8, NZ), F32),
            pltpu.VMEM((NX, 8, NZ), F32),
            pltpu.SemaphoreType.DMA((12,)),
        ],
        compiler_params=params(),
        name="messages",
    )(vs, c)


def y_halo(even, one, two, first, size, before):
    rows = slice(first, first + size)
    return jnp.where(even == before, two[rows], one[rows])


def corner_kernel(ya, yb, _, one, two):
    even_x = is_even("gx")
    even_y = is_even("gy")
    inside_x = jnp.where(at_end("gx"), 0.0, 1.0)
    blank = jnp.zeros((2, NZ), F32)
    for i in range(13):
        if i < 9:
            k, layer = divmod(i, 3)
            size, places = 3, (9 * layer + 3 * k, 9 * (NX - 3 + layer) + 3 * k)
            one[i, 3:5] = blank
            two[i, 3:5] = blank
        else:
            size, places = 4, (SLAB_V + 4 * (i - 9), SLAB_V + 4 * (NX - 4 + i - 9))
        for spot, before in ((slice(0, size), False), (slice(8 - size, 8), True)):
            low, high = (y_halo(even_y, ya, yb, row, size, before) for row in places)
            one[i, spot] = jnp.where(even_x, high, low)
            two[i, spot] = jnp.where(even_x, low, high) * inside_x


def corners(ya, yb, meta):
    shape = jax.ShapeDtypeStruct((13, 8, NZ), F32)
    return pl.pallas_call(
        corner_kernel,
        out_shape=(shape, shape),
        in_specs=[vmem()] * 3,
        out_specs=(vmem(), vmem()),
        compiler_params=params(),
        name="corners",
    )(ya, yb, meta)


def route_kernel(patch, spans, par, to_patch, to_slot, meta):
    patch_row = patch[...]
    hot = (lax.broadcasted_iota(jnp.int32, (DEV, ROWS), 0) == patch_row).astype(F32)
    hot16 = hot.astype(BF16)
    to_patch[...] = hot16
    upper = (
        lax.broadcasted_iota(jnp.int32, (128, 128), 0)
        <= lax.broadcasted_iota(jnp.int32, (128, 128), 1)
    ).astype(BF16)
    before = jnp.zeros((DEV, 1), F32)
    ranks = []
    for block in range(ROWS // 128):
        part = slice(128 * block, 128 * block + 128)
        count = dot(hot16[:, part], upper) + before
        ranks.append(jnp.sum(count * hot[:, part], axis=0, keepdims=True) - 1.0)
        before = count[:, 127:128]
    rank = jnp.concatenate(ranks, axis=1)
    slot_hot = (lax.broadcasted_iota(jnp.int32, (CAP, ROWS), 0).astype(F32) == rank).astype(F32)
    to_slot[...] = slot_hot
    fields = [
        spans[0:1].astype(F32),
        spans[1:2].astype(F32),
        par[0:1],
        par[1:2],
    ]
    spread = jnp.concatenate(
        [slot_hot * field for field in fields], axis=0
    )
    high, mid, low = three_pieces(spread)
    meta[...] = dot_nt(hot16, high) + dot_nt(hot16, mid) + dot_nt(hot16, low)


def route(patch, spans, par):
    return pl.pallas_call(
        route_kernel,
        out_shape=(
            jax.ShapeDtypeStruct((DEV, ROWS), BF16),
            jax.ShapeDtypeStruct((CAP, ROWS), F32),
            jax.ShapeDtypeStruct((DEV, 128), F32),
        ),
        in_specs=[vmem()] * 3,
        out_specs=(vmem(),) * 3,
        compiler_params=params(),
        cost_estimate=pl.CostEstimate(flops=400_000_000, bytes_accessed=2_000_000, transcendentals=0),
        name="route",
    )(patch, spans, par)


def up(x):
    return pltpu.roll(x, x.shape[0] - 1, 0)


def down(x):
    return pltpu.roll(x, 1, 0)


class Rows:
    def __init__(self):
        self.place = {}

    def hold(self, ref, rows):
        for index, x in enumerate(rows):
            self.place[x] = (ref, index)
        return self

    def __getitem__(self, x):
        ref, index = self.place[x]
        return ref[index]

    def __setitem__(self, x, value):
        ref, index = self.place[x]
        ref[index] = value


EDGE = [4, 5, 6, 7, 8, 31, 32, 33, 34, 35]
MIDDLE = list(range(9, 31))


class Stencil:
    def __init__(self, stiff, ratio, wx, wy, wz, scale, y0, y1, y2):
        self.stiff, self.ratio, self.scale = stiff, ratio, scale
        self.wx, self.wy, self.wz = wx, wy, wz
        self.fields = (y0, y1, y2)
        lane = lax.broadcasted_iota(jnp.int32, (EY, NZ), 1)
        self.not_last = lane < NZ - 1
        self.not_first = lane > 0

    def prepare(self, x, source):
        here, after, before = self.stiff[x], self.stiff[x + 1], self.stiff[x - 1]
        y_next = up(here)
        z_next = jnp.where(self.not_last, pltpu.roll(here, NZ - 1, 1), 0.0)
        z_prev = jnp.where(self.not_first, pltpu.roll(here, 1, 1), 0.0)
        sides = (before + after) + (y_next + down(here)) + (z_next + z_prev)
        diag = 3.0 * here + 0.5 * sides
        inverse = jnp.where(here > 0.0, 1.0 / diag, 0.0)
        self.ratio[x] = OMEGA * inverse
        self.wx[x] = 0.5 * (here + after)
        self.wy[x] = 0.5 * (here + y_next)
        self.wz[x] = jnp.where(self.not_last, 0.5 * (here + z_next), 0.0)
        self.scale[x] = diag
        for k in range(3):
            self.fields[0][k][x] = source(k, x) * inverse

    def update(self, level, k, x):
        source = self.fields[level][k]
        here = source[x]
        face_y, face_z = self.wy[x], self.wz[x]
        total = self.wx[x] * source[x + 1] + self.wx[x - 1] * source[x - 1]
        total = total + (face_y * up(here) + down(face_y * here))
        total = total + (
            face_z * pltpu.roll(here, NZ - 1, 1) + pltpu.roll(face_z * here, 1, 1)
        )
        return self.fields[0][k][x] + KEEP * here + self.ratio[x] * total

    def sweep(self, level, rows):
        for x in rows:
            for k in range(3):
                self.fields[level + 1][k][x] = self.update(level, k, x)

    def finish(self, x, out, surface, index):
        for k in range(3):
            fresh = self.update(2, k, x)[0:NY]
            surface[k, index] = fresh
            out[k, index] = fresh * self.scale[x][0:NY]


def interior_kernel(
    vs, c, ya, yb, out, surface, keep, keep3, stiff, mids, mids3,
):
    even_y = is_even("gy")
    for x in range(NX):
        row = SLAB_V + 4 * x
        stiff[x, 0:NY] = c[x]
        stiff[x, NY : NY + 4] = y_halo(even_y, ya, yb, row, 4, False)
        stiff[x, EY - 4 : EY] = y_halo(even_y, ya, yb, row, 4, True)
    for x in range(1, NX - 1):
        for k in range(3):
            row = 9 * x + 3 * k
            place = (keep3.at[0, k], EDGE.index(x + 4)) if x + 4 in EDGE else (mids3.at[0, k], x - 5)
            ref, index = place
            ref[index, NY : NY + 3] = y_halo(even_y, ya, yb, row, 3, False)
            ref[index, EY - 3 : EY] = y_halo(even_y, ya, yb, row, 3, True)

    def source(k, x):
        ref, index = fields[0][k].place[x]
        return jnp.concatenate([vs[k, x - 4], ref[index, NY:EY]], axis=0)

    def plane(n):
        return Rows().hold(keep.at[n], EDGE).hold(mids.at[n], MIDDLE)

    fields = [
        [Rows().hold(keep3.at[n, k], EDGE).hold(mids3.at[n, k], MIDDLE) for k in range(3)]
        for n in range(3)
    ]
    grid = Stencil(
        Rows().hold(stiff, range(4, 36)), plane(0), plane(1), plane(2), plane(3), plane(4), *fields
    )
    for x in (4, 5, 34, 35):
        keep[5, EDGE.index(x)] = grid.stiff[x]
    for x in range(5, 35):
        grid.prepare(x, source)
    grid.sweep(0, range(6, 34))
    grid.sweep(1, range(7, 33))
    for x in range(8, 32):
        grid.finish(x, out, surface, x - 8)


def interior(vs, c, ya, yb):
    rows = jax.ShapeDtypeStruct((3, 24, NY, NZ), F32)
    return pl.pallas_call(
        interior_kernel,
        out_shape=(
            rows,
            rows,
            jax.ShapeDtypeStruct((6, len(EDGE), EY, NZ), F32),
            jax.ShapeDtypeStruct((3, 3, len(EDGE), EY, NZ), F32),
        ),
        in_specs=[vmem()] * 4,
        out_specs=(vmem(),) * 4,
        scratch_shapes=[
            pltpu.VMEM((NX, EY, NZ), F32),
            pltpu.VMEM((5, len(MIDDLE), EY, NZ), F32),
            pltpu.VMEM((3, 3, len(MIDDLE), EY, NZ), F32),
        ],
        compiler_params=params(),
        cost_estimate=pl.CostEstimate(flops=60_000_000, bytes_accessed=6_000_000, transcendentals=0),
        name="interior",
    )(vs, c, ya, yb)


def edge_kernel(
    vs, ya, yb, xa, xb, za, zb, keep, keep3, out, surface, fresh, fresh3,
):
    even_x = is_even("gx")
    even_y = is_even("gy")

    def x_halo(layer, before):
        center = jnp.where(even_x == before, xb[layer], xa[layer])
        corner = jnp.where(even_x == before, zb[layer], za[layer])
        return jnp.concatenate([center, corner], axis=0)

    class Given:
        def __getitem__(self, x):
            if x < 4:
                return x_halo(9 + x, True)
            if x < 36:
                return keep[5, EDGE.index(x)]
            return x_halo(9 + x - 36, False)

    def source(k, x):
        if x == 4 or x == 35:
            spot = 0 if x == 4 else 1
            row = 9 * (x - 4) + 3 * k
            fresh3[3, k, spot, NY : NY + 3] = y_halo(even_y, ya, yb, row, 3, False)
            fresh3[3, k, spot, EY - 3 : EY] = y_halo(even_y, ya, yb, row, 3, True)
            return jnp.concatenate([vs[k, x - 4], fresh3[3, k, spot, NY:EY]], axis=0)
        if x < 4:
            return x_halo(3 * k + x - 1, True)
        return x_halo(3 * k + x - 36, False)

    def hold(ref3, n, k, rows):
        return Rows().hold(keep3.at[n, k], EDGE).hold(ref3.at[n, k], rows)

    first = [1, 2, 3, 4, 35, 36, 37, 38]
    second = [2, 3, 4, 5, 34, 35, 36, 37]
    third = [3, 4, 5, 6, 33, 34, 35, 36]
    last = [4, 5, 6, 7, 32, 33, 34, 35]
    planes = [Rows().hold(keep.at[n], EDGE).hold(fresh.at[n], first) for n in range(5)]
    fields = [
        [hold(fresh3, n, k, rows) for k in range(3)] for n, rows in enumerate((first, second, third))
    ]
    grid = Stencil(Given(), *planes, *fields)
    for x in first:
        grid.prepare(x, source)
    grid.sweep(0, second)
    grid.sweep(1, third)
    for index, x in enumerate(last):
        grid.finish(x, out, surface, index)


def edges(vs, ya, yb, xa, xb, za, zb, keep, keep3):
    rows = jax.ShapeDtypeStruct((3, 8, NY, NZ), F32)
    return pl.pallas_call(
        edge_kernel,
        out_shape=(rows, rows),
        in_specs=[vmem()] * 9,
        out_specs=(vmem(),) * 2,
        scratch_shapes=[
            pltpu.VMEM((5, 8, EY, NZ), F32),
            pltpu.VMEM((4, 3, 8, EY, NZ), F32),
        ],
        compiler_params=params(),
        cost_estimate=pl.CostEstimate(flops=20_000_000, bytes_accessed=2_000_000, transcendentals=0),
        name="edges",
    )(vs, ya, yb, xa, xb, za, zb, keep, keep3)


def pack_kernel(to_patch, to_slot, meta, outer, inner, send):
    column = lax.broadcasted_iota(jnp.int32, (DEV, NZ), 1)
    values = []
    for block in range(ROWS // DEV):
        if block == 0:
            ref, part = outer, slice(0, 4)
        elif block == 7:
            ref, part = outer, slice(4, 8)
        else:
            ref, part = inner, slice(4 * block - 4, 4 * block)
        first, second, third = (ref[k, part].reshape(DEV, NZ) for k in range(3))
        mixed = jnp.where(column == 1, pltpu.roll(second, 1, 1), first)
        mixed = jnp.where(column == 2, pltpu.roll(third, 2, 1), mixed)
        values.append(OMEGA * mixed.T[0:3])
    values = jnp.concatenate(values, axis=1)
    slots = to_slot[...]
    spread = jnp.concatenate([slots * values[k : k + 1] for k in range(3)], axis=0)
    sent = dot_nt(jnp.concatenate(three_pieces(spread), axis=0), to_patch[...])
    sent = sent[0:96] + sent[96:192] + sent[192:288]
    send[:, 0:128] = meta[...]
    send[:, 128:256] = jnp.concatenate([sent, jnp.zeros((CAP, DEV), F32)], axis=0).T


def pack(to_patch, to_slot, meta, outer, inner):
    return pl.pallas_call(
        pack_kernel,
        out_shape=jax.ShapeDtypeStruct((DEV, 256), F32),
        in_specs=[vmem()] * 5,
        out_specs=vmem(),
        compiler_params=params(),
        name="pack",
    )(to_patch, to_slot, meta, outer, inner)


def pieces(param):
    other = 1.0 - param
    return [
        other * other * other / 6.0,
        (3.0 * param * param * param - 6.0 * param * param + 4.0) / 6.0,
        (-3.0 * param * param * param + 3.0 * param * param + 3.0 * param + 1.0) / 6.0,
        param * param * param / 6.0,
    ]


def gather_kernel(got, inner, outer, field, grads, table, left, right, sems):
    writes = [
        pltpu.make_async_copy(inner, field.at[:, 4:28], sems.at[0]),
        pltpu.make_async_copy(outer.at[:, 0:4], field.at[:, 0:4], sems.at[1]),
        pltpu.make_async_copy(outer.at[:, 4:8], field.at[:, 28:32], sems.at[2]),
    ]
    for write in writes:
        write.start()
    table[0:128] = got[:, 0:128].T
    table[128:256] = got[:, 128:256].T
    basis_u = pieces(table[64:96])
    basis_v = pieces(table[96:128])
    knot = lax.broadcasted_iota(jnp.int32, (NC, DEV), 0).astype(F32)

    def spline(span, basis, slot):
        offset = knot - table[span + slot : span + slot + 1]
        rows = jnp.zeros((NC, DEV), F32)
        for index in range(4):
            rows = jnp.where(offset == float(index), basis[index][slot : slot + 1], rows)
        return rows

    product = jnp.zeros((6 * NC, 2 * NC), F32)
    for slot in range(CAP):
        part = slice(DEV * slot, DEV * slot + DEV)
        along_u = spline(0, basis_u, slot)
        for k in range(3):
            value = table[128 + CAP * k + slot : 128 + CAP * k + slot + 1]
            high, low = two_pieces(along_u * value)
            left[NC * k : NC * k + NC, part] = high
            left[3 * NC + NC * k : 3 * NC + NC * k + NC, part] = low
        high, low = two_pieces(spline(CAP, basis_v, slot))
        right[0:NC, part] = high
        right[NC : 2 * NC, part] = low
        if slot % CHUNK == CHUNK - 1:
            block = slice(DEV * (slot + 1 - CHUNK), DEV * (slot + 1))
            product = product + dot_nt(left[:, block], right[:, block])
    total = product[0 : 3 * NC, 0:NC] + (
        product[0 : 3 * NC, NC : 2 * NC] + product[3 * NC : 6 * NC, 0:NC]
    )
    grads[0] = total.reshape(3, NC, NC)
    for write in writes:
        write.wait()


def gather(got, inner, outer):
    return pl.pallas_call(
        gather_kernel,
        out_shape=(
            jax.ShapeDtypeStruct((3, NX, NY, NZ), F32),
            jax.ShapeDtypeStruct((1, 3, NC, NC), F32),
        ),
        in_specs=[vmem()] * 3,
        out_specs=(pl.BlockSpec(memory_space=pl.ANY), vmem()),
        scratch_shapes=[
            pltpu.VMEM((256, DEV), F32),
            pltpu.VMEM((6 * NC, DEV * CAP), BF16),
            pltpu.VMEM((2 * NC, DEV * CAP), BF16),
            pltpu.SemaphoreType.DMA((3,)),
        ],
        compiler_params=params(),
        cost_estimate=pl.CostEstimate(flops=400_000_000, bytes_accessed=200_000, transcendentals=0),
        name="gather",
    )(got, inner, outer)


def body(volume_sens, stiffness, patch_of_row, knot_spans, span_params):
    y_one, y_two, x_one, x_two = messages(
        pltpu.with_memory_space_constraint(volume_sens, pltpu.HBM),
        pltpu.with_memory_space_constraint(stiffness, pltpu.HBM),
    )
    ya, yb = exchange(False, y_one, y_two)
    xa, xb = exchange(True, x_one, x_two)
    to_patch, to_slot, meta = route(
        patch_of_row.reshape(1, ROWS), knot_spans[0].T, span_params[0].T
    )
    za, zb = exchange(True, *corners(ya, yb, meta))
    inner, inner_surface, keep, keep3 = interior(volume_sens, stiffness, ya, yb)
    outer, outer_surface = edges(volume_sens, ya, yb, xa, xb, za, zb, keep, keep3)
    send = pack(to_patch, to_slot, meta, outer_surface, inner_surface)
    got = lax.all_to_all(send, ("gx", "gy"), 0, 0, tiled=True)
    return gather(got, inner, outer)


def solution(mesh):
    placed = (
        P(None, "gx", "gy", None),
        P("gx", "gy", None),
        P(("gx", "gy"), None, None),
        P(("gx", "gy"), None, None),
        P(("gx", "gy"), None, None),
    )
    return jax.shard_map(
        body,
        mesh=mesh,
        in_specs=placed,
        out_specs=(P(None, "gx", "gy", None), P(("gx", "gy"), None, None, None)),
        check_vma=False,
    )
```

```python
import jax
import jax.numpy as jnp
from jax import lax
from jax.experimental import pallas as pl
from jax.experimental.pallas import tpu as pltpu
from jax.sharding import PartitionSpec as P

NC = 64
OMEGA = 2.0 / 3.0
KEEP = 1.0 - OMEGA
NX = 32
NY = 32
NZ = 128
ROWS = NX * NY
CAP = 32
DEV = 128
CHUNK = 8
EX = NX + 8
EY = NY + 8
SLAB_V = 9 * NX
SLAB = 13 * NX
F32 = jnp.float32
BF16 = jnp.bfloat16
VMEM_LIMIT = 24 * 1024 * 1024


def vmem():
    return pl.BlockSpec(memory_space=pltpu.VMEM)


def params():
    return pltpu.CompilerParams(vmem_limit_bytes=VMEM_LIMIT)


def is_even(axis):
    return lax.rem(lax.axis_index(axis), 2) == 0


def exchange(along_x, one, two):
    count_x, count_y = lax.axis_size("gx"), lax.axis_size("gy")

    def partner(i, last):
        return i if i in (0, last) else ((i + 1) ^ 1) - 1

    first, second = [], []
    for i in range(count_x):
        for j in range(count_y):
            if along_x:
                near, far = (i ^ 1, j), (partner(i, count_x - 1), j)
                far = (count_x - 1 - i, j) if far == (i, j) else far
            else:
                near, far = (i, j ^ 1), (i, partner(j, count_y - 1))
                far = (i ^ 1, j) if far == (i, j) else far
            here = i * count_y + j
            first.append((here, near[0] * count_y + near[1]))
            second.append((here, far[0] * count_y + far[1]))
    both = ("gx", "gy")
    return lax.ppermute(one, both, first), lax.ppermute(two, both, second)


def at_end(axis):
    here = lax.axis_index(axis)
    return jnp.logical_or(here == 0, here == lax.axis_size(axis) - 1)


def two_pieces(x):
    high = x.astype(BF16)
    return high, (x - high.astype(F32)).astype(BF16)


def three_pieces(x):
    high = x.astype(BF16)
    rest = x - high.astype(F32)
    mid = rest.astype(BF16)
    return high, mid, (rest - mid.astype(F32)).astype(BF16)


def dot(a, b):
    return jnp.dot(a, b, preferred_element_type=F32)


def dot_nt(a, b):
    return lax.dot_general(a, b, (((1,), (1,)), ((), ())), preferred_element_type=F32)


def message_kernel(vs, c, y_one, y_two, x_one, x_two, low_v, high_v, low_c, high_c, sems):
    slabs = [
        pltpu.make_async_copy(vs.at[:, :, 0:8], low_v, sems.at[0]),
        pltpu.make_async_copy(vs.at[:, :, NY - 8 : NY], high_v, sems.at[1]),
        pltpu.make_async_copy(c.at[:, 0:8], low_c, sems.at[2]),
        pltpu.make_async_copy(c.at[:, NY - 8 : NY], high_c, sems.at[3]),
    ]
    for copy in slabs:
        copy.start()

    def layers(low, high):
        copies = []
        for k in range(3):
            spot = slice(3 * k, 3 * k + 3)
            copies.append(pltpu.make_async_copy(vs.at[k, 0:3], low.at[spot], sems.at[4 + k]))
            copies.append(
                pltpu.make_async_copy(vs.at[k, NX - 3 : NX], high.at[spot], sems.at[7 + k])
            )
        copies.append(pltpu.make_async_copy(c.at[0:4], low.at[9:13], sems.at[10]))
        copies.append(pltpu.make_async_copy(c.at[NX - 4 : NX], high.at[9:13], sems.at[11]))
        return copies

    even_x = is_even("gx")
    even_y = is_even("gy")

    @pl.when(even_x)
    def _():
        for copy in layers(x_two, x_one):
            copy.start()

    @pl.when(jnp.logical_not(even_x))
    def _():
        for copy in layers(x_one, x_two):
            copy.start()

    inside_y = jnp.where(at_end("gy"), 0.0, 1.0)

    def put(row, size, low, high):
        y_one[row : row + size] = jnp.where(even_y, high, low)
        y_two[row : row + size] = jnp.where(even_y, low, high) * inside_y

    for copy in slabs:
        copy.wait()
    for x in range(NX):
        for k in range(3):
            put(9 * x + 3 * k, 3, low_v[k, x, 0:3], high_v[k, x, 5:8])
        put(SLAB_V + 4 * x, 4, low_c[x, 0:4], high_c[x, 4:8])

    @pl.when(even_x)
    def _():
        for copy in layers(x_two, x_one):
            copy.wait()

    @pl.when(jnp.logical_not(even_x))
    def _():
        for copy in layers(x_one, x_two):
            copy.wait()

    @pl.when(at_end("gx"))
    def _():
        x_two[...] = jnp.zeros((13, NY, NZ), F32)


def messages(vs, c):
    y_shape = jax.ShapeDtypeStruct((SLAB, NZ), F32)
    x_shape = jax.ShapeDtypeStruct((13, NY, NZ), F32)
    return pl.pallas_call(
        message_kernel,
        out_shape=(y_shape, y_shape, x_shape, x_shape),
        in_specs=[pl.BlockSpec(memory_space=pltpu.HBM)] * 2,
        out_specs=(vmem(),) * 4,
        scratch_shapes=[
            pltpu.VMEM((3, NX, 8, NZ), F32),
            pltpu.VMEM((3, NX, 8, NZ), F32),
            pltpu.VMEM((NX, 8, NZ), F32),
            pltpu.VMEM((NX, 8, NZ), F32),
            pltpu.SemaphoreType.DMA((12,)),
        ],
        compiler_params=params(),
        name="messages",
    )(vs, c)


def y_halo(even, one, two, first, size, before):
    rows = slice(first, first + size)
    return jnp.where(even == before, two[rows], one[rows])


def corner_kernel(ya, yb, _, __, one, two):
    even_x = is_even("gx")
    even_y = is_even("gy")
    inside_x = jnp.where(at_end("gx"), 0.0, 1.0)
    blank = jnp.zeros((2, NZ), F32)
    for i in range(13):
        if i < 9:
            k, layer = divmod(i, 3)
            size, places = 3, (9 * layer + 3 * k, 9 * (NX - 3 + layer) + 3 * k)
            one[i, 3:5] = blank
            two[i, 3:5] = blank
        else:
            size, places = 4, (SLAB_V + 4 * (i - 9), SLAB_V + 4 * (NX - 4 + i - 9))
        for spot, before in ((slice(0, size), False), (slice(8 - size, 8), True)):
            low, high = (y_halo(even_y, ya, yb, row, size, before) for row in places)
            one[i, spot] = jnp.where(even_x, high, low)
            two[i, spot] = jnp.where(even_x, low, high) * inside_x


def corners(ya, yb, meta, early):
    shape = jax.ShapeDtypeStruct((13, 8, NZ), F32)
    return pl.pallas_call(
        corner_kernel,
        out_shape=(shape, shape),
        in_specs=[vmem()] * 4,
        out_specs=(vmem(), vmem()),
        compiler_params=params(),
        name="corners",
    )(ya, yb, meta, early)


def route_kernel(patch, spans, par, to_patch, to_slot, meta):
    patch_row = patch[...]
    hot = (lax.broadcasted_iota(jnp.int32, (DEV, ROWS), 0) == patch_row).astype(F32)
    hot16 = hot.astype(BF16)
    to_patch[...] = hot16
    upper = (
        lax.broadcasted_iota(jnp.int32, (128, 128), 0)
        <= lax.broadcasted_iota(jnp.int32, (128, 128), 1)
    ).astype(BF16)
    before = jnp.zeros((DEV, 1), F32)
    ranks = []
    for block in range(ROWS // 128):
        part = slice(128 * block, 128 * block + 128)
        count = dot(hot16[:, part], upper) + before
        ranks.append(jnp.sum(count * hot[:, part], axis=0, keepdims=True) - 1.0)
        before = count[:, 127:128]
    rank = jnp.concatenate(ranks, axis=1)
    slot_hot = (lax.broadcasted_iota(jnp.int32, (CAP, ROWS), 0).astype(F32) == rank).astype(F32)
    to_slot[...] = slot_hot
    fields = [
        spans[0:1].astype(F32),
        spans[1:2].astype(F32),
        par[0:1],
        par[1:2],
    ]
    spread = jnp.concatenate(
        [slot_hot * field for field in fields], axis=0
    )
    high, mid, low = three_pieces(spread)
    meta[...] = dot_nt(hot16, high) + dot_nt(hot16, mid) + dot_nt(hot16, low)


def route(patch, spans, par):
    return pl.pallas_call(
        route_kernel,
        out_shape=(
            jax.ShapeDtypeStruct((DEV, ROWS), BF16),
            jax.ShapeDtypeStruct((CAP, ROWS), F32),
            jax.ShapeDtypeStruct((DEV, 128), F32),
        ),
        in_specs=[vmem()] * 3,
        out_specs=(vmem(),) * 3,
        compiler_params=params(),
        cost_estimate=pl.CostEstimate(flops=400_000_000, bytes_accessed=2_000_000, transcendentals=0),
        name="route",
    )(patch, spans, par)


def up(x):
    return pltpu.roll(x, x.shape[0] - 1, 0)


def down(x):
    return pltpu.roll(x, 1, 0)


class Rows:
    def __init__(self):
        self.place = {}

    def hold(self, ref, rows):
        for index, x in enumerate(rows):
            self.place[x] = (ref, index)
        return self

    def __getitem__(self, x):
        ref, index = self.place[x]
        return ref[index]

    def __setitem__(self, x, value):
        ref, index = self.place[x]
        ref[index] = value


EDGE = [4, 5, 6, 7, 8, 31, 32, 33, 34, 35]
MIDDLE = list(range(9, 31))


class Joined:
    def __init__(self, whole, rest, ahead):
        self.whole, self.rest, self.ahead = whole, rest, ahead

    def __getitem__(self, x):
        if x in EDGE:
            return self.whole[EDGE.index(x)]
        spot = MIDDLE.index(x)
        return jnp.concatenate(
            [self.rest[spot, 16:24], self.ahead[x - 5, 8:24], self.rest[spot, 0:16]], axis=0
        )

    def __setitem__(self, x, value):
        if x in EDGE:
            spot = EDGE.index(x)
            self.whole[spot, 24:40] = value[0:16]
            self.whole[spot, 8:24] = self.ahead[x - 5, 8:24]
            self.whole[spot, 0:8] = value[16:24]
        else:
            self.rest[MIDDLE.index(x)] = value


def all_rows(v):
    return v


def outer_rows(v):
    return jnp.concatenate([v[24:40], v[0:8]], axis=0)


def last_outer_rows(v):
    return jnp.concatenate([v[24:32], v[0:8]], axis=0)


def inner_rows(v):
    return v[8:24]


def center_rows(v):
    return v[0:NY]


class Stencil:
    def __init__(self, part, last_part, height, stiff, ratio, wx, wy, wz, scale, y0, y1, y2):
        self.part, self.last_part = part, last_part
        self.stiff, self.ratio, self.scale = stiff, ratio, scale
        self.wx, self.wy, self.wz = wx, wy, wz
        self.fields = (y0, y1, y2)
        lane = lax.broadcasted_iota(jnp.int32, (height, NZ), 1)
        self.not_last = lane < NZ - 1
        self.not_first = lane > 0

    def prepare(self, x, source):
        part = self.part
        whole = self.stiff[x]
        here, after, before = part(whole), part(self.stiff[x + 1]), part(self.stiff[x - 1])
        y_next = part(up(whole))
        z_next = jnp.where(self.not_last, pltpu.roll(here, NZ - 1, 1), 0.0)
        z_prev = jnp.where(self.not_first, pltpu.roll(here, 1, 1), 0.0)
        sides = (before + after) + (y_next + part(down(whole))) + (z_next + z_prev)
        diag = 3.0 * here + 0.5 * sides
        inverse = jnp.where(here > 0.0, 1.0 / diag, 0.0)
        self.ratio[x] = OMEGA * inverse
        self.wx[x] = 0.5 * (here + after)
        self.wy[x] = 0.5 * (here + y_next)
        self.wz[x] = jnp.where(self.not_last, 0.5 * (here + z_next), 0.0)
        self.scale[x] = diag
        for k in range(3):
            self.fields[0][k][x] = source(k, x) * inverse

    def update(self, level, k, x, part):
        source = self.fields[level][k]
        whole, face_y = source[x], self.wy[x]
        here, face_z = part(whole), part(self.wz[x])
        total = part(self.wx[x]) * part(source[x + 1]) + part(self.wx[x - 1]) * part(source[x - 1])
        total = total + (part(face_y) * part(up(whole)) + part(down(face_y * whole)))
        total = total + (
            face_z * pltpu.roll(here, NZ - 1, 1) + pltpu.roll(face_z * here, 1, 1)
        )
        return part(self.fields[0][k][x]) + KEEP * here + part(self.ratio[x]) * total

    def sweep(self, level, rows):
        for x in rows:
            for k in range(3):
                self.fields[level + 1][k][x] = self.update(level, k, x, self.part)

    def finish(self, x, out, surface, index):
        for k in range(3):
            fresh = self.update(2, k, x, self.last_part)
            surface[k, index] = fresh
            out[k, index] = fresh * self.last_part(self.scale[x])


PREPARED = list(range(5, 35))


def ahead_kernel(vs, c, out, surface, planes, cubes):
    class Given:
        def __getitem__(self, x):
            return c[x - 4]

    fields = [[Rows().hold(cubes.at[n, k], PREPARED) for k in range(3)] for n in range(3)]
    grid = Stencil(
        all_rows, inner_rows, NY, Given(),
        *(Rows().hold(planes.at[n], PREPARED) for n in range(5)), *fields,
    )
    for x in range(5, 35):
        grid.prepare(x, lambda k, x: vs[k, x - 4])
    grid.sweep(0, range(6, 34))
    grid.sweep(1, range(7, 33))
    for x in range(8, 32):
        grid.finish(x, out, surface, x - 8)


def ahead(vs, c):
    rows = jax.ShapeDtypeStruct((3, 24, 16, NZ), F32)
    return pl.pallas_call(
        ahead_kernel,
        out_shape=(
            rows,
            rows,
            jax.ShapeDtypeStruct((5, len(PREPARED), NY, NZ), F32),
            jax.ShapeDtypeStruct((3, 3, len(PREPARED), NY, NZ), F32),
        ),
        in_specs=[vmem()] * 2,
        out_specs=(vmem(),) * 4,
        compiler_params=params(),
        cost_estimate=pl.CostEstimate(flops=60_000_000, bytes_accessed=6_000_000, transcendentals=0),
        name="ahead",
    )(vs, c)


def interior_kernel(
    vs, c, ya, yb, planes, cubes, out, surface, keep, keep3, stiff, rest, rest3, halo,
):
    even_y = is_even("gy")
    for x in range(NX):
        row = SLAB_V + 4 * x
        stiff[x, 0:NY] = c[x]
        stiff[x, NY : NY + 4] = y_halo(even_y, ya, yb, row, 4, False)
        stiff[x, EY - 4 : EY] = y_halo(even_y, ya, yb, row, 4, True)
    for x in range(1, NX - 1):
        for k in range(3):
            row = 9 * x + 3 * k
            halo[k, x, 0:3] = y_halo(even_y, ya, yb, row, 3, False)
            halo[k, x, 5:8] = y_halo(even_y, ya, yb, row, 3, True)

    def source(k, x):
        return jnp.concatenate([vs[k, x - 4, 24:32], halo[k, x - 4], vs[k, x - 4, 0:8]], axis=0)

    fields = [
        [Joined(keep3.at[n, k], rest3.at[n, k], cubes.at[n, k]) for k in range(3)] for n in range(3)
    ]
    grid = Stencil(
        outer_rows, last_outer_rows, 24, Rows().hold(stiff, range(4, 36)),
        *(Joined(keep.at[n], rest.at[n], planes.at[n]) for n in range(5)), *fields,
    )
    for x in (4, 5, 34, 35):
        keep[5, EDGE.index(x)] = grid.stiff[x]
    for x in range(5, 35):
        grid.prepare(x, source)
    grid.sweep(0, range(6, 34))
    grid.sweep(1, range(7, 33))
    for x in range(8, 32):
        grid.finish(x, out, surface, x - 8)


def interior(vs, c, ya, yb, planes, cubes):
    rows = jax.ShapeDtypeStruct((3, 24, 16, NZ), F32)
    return pl.pallas_call(
        interior_kernel,
        out_shape=(
            rows,
            rows,
            jax.ShapeDtypeStruct((6, len(EDGE), EY, NZ), F32),
            jax.ShapeDtypeStruct((3, 3, len(EDGE), EY, NZ), F32),
        ),
        in_specs=[vmem()] * 6,
        out_specs=(vmem(),) * 4,
        scratch_shapes=[
            pltpu.VMEM((NX, EY, NZ), F32),
            pltpu.VMEM((5, len(MIDDLE), 24, NZ), F32),
            pltpu.VMEM((3, 3, len(MIDDLE), 24, NZ), F32),
            pltpu.VMEM((3, NX, 8, NZ), F32),
        ],
        compiler_params=params(),
        cost_estimate=pl.CostEstimate(flops=60_000_000, bytes_accessed=6_000_000, transcendentals=0),
        name="interior",
    )(vs, c, ya, yb, planes, cubes)


def edge_kernel(
    vs, ya, yb, xa, xb, za, zb, keep, keep3, out, surface, fresh, fresh3,
):
    even_x = is_even("gx")
    even_y = is_even("gy")

    def x_halo(layer, before):
        center = jnp.where(even_x == before, xb[layer], xa[layer])
        corner = jnp.where(even_x == before, zb[layer], za[layer])
        return jnp.concatenate([center, corner], axis=0)

    class Given:
        def __getitem__(self, x):
            if x < 4:
                return x_halo(9 + x, True)
            if x < 36:
                return keep[5, EDGE.index(x)]
            return x_halo(9 + x - 36, False)

    def source(k, x):
        if x == 4 or x == 35:
            spot = 0 if x == 4 else 1
            row = 9 * (x - 4) + 3 * k
            fresh3[3, k, spot, NY : NY + 3] = y_halo(even_y, ya, yb, row, 3, False)
            fresh3[3, k, spot, EY - 3 : EY] = y_halo(even_y, ya, yb, row, 3, True)
            return jnp.concatenate([vs[k, x - 4], fresh3[3, k, spot, NY:EY]], axis=0)
        if x < 4:
            return x_halo(3 * k + x - 1, True)
        return x_halo(3 * k + x - 36, False)

    def hold(ref3, n, k, rows):
        return Rows().hold(keep3.at[n, k], EDGE).hold(ref3.at[n, k], rows)

    first = [1, 2, 3, 4, 35, 36, 37, 38]
    second = [2, 3, 4, 5, 34, 35, 36, 37]
    third = [3, 4, 5, 6, 33, 34, 35, 36]
    last = [4, 5, 6, 7, 32, 33, 34, 35]
    planes = [Rows().hold(keep.at[n], EDGE).hold(fresh.at[n], first) for n in range(5)]
    fields = [
        [hold(fresh3, n, k, rows) for k in range(3)] for n, rows in enumerate((first, second, third))
    ]
    grid = Stencil(all_rows, center_rows, EY, Given(), *planes, *fields)
    for x in first:
        grid.prepare(x, source)
    grid.sweep(0, second)
    grid.sweep(1, third)
    for index, x in enumerate(last):
        grid.finish(x, out, surface, index)


def edges(vs, ya, yb, xa, xb, za, zb, keep, keep3):
    rows = jax.ShapeDtypeStruct((3, 8, NY, NZ), F32)
    return pl.pallas_call(
        edge_kernel,
        out_shape=(rows, rows),
        in_specs=[vmem()] * 9,
        out_specs=(vmem(),) * 2,
        scratch_shapes=[
            pltpu.VMEM((5, 8, EY, NZ), F32),
            pltpu.VMEM((4, 3, 8, EY, NZ), F32),
        ],
        compiler_params=params(),
        cost_estimate=pl.CostEstimate(flops=20_000_000, bytes_accessed=2_000_000, transcendentals=0),
        name="edges",
    )(vs, ya, yb, xa, xb, za, zb, keep, keep3)


def pack_kernel(to_patch, to_slot, meta, outer, inner, early, send):
    column = lax.broadcasted_iota(jnp.int32, (DEV, NZ), 1)
    values = []
    for block in range(ROWS // DEV):
        pieces_of = [[], [], []]
        for k in range(3):
            for x in range(4 * block, 4 * block + 4):
                if 4 <= x < 28:
                    pieces_of[k] += [inner[k, x - 4, 8:16], early[k, x - 4], inner[k, x - 4, 0:8]]
                else:
                    pieces_of[k].append(outer[k, x if x < 4 else x - 24])
        first, second, third = (jnp.concatenate(p, axis=0) for p in pieces_of)
        mixed = jnp.where(column == 1, pltpu.roll(second, 1, 1), first)
        mixed = jnp.where(column == 2, pltpu.roll(third, 2, 1), mixed)
        values.append(OMEGA * mixed.T[0:3])
    values = jnp.concatenate(values, axis=1)
    slots = to_slot[...]
    spread = jnp.concatenate([slots * values[k : k + 1] for k in range(3)], axis=0)
    sent = dot_nt(jnp.concatenate(three_pieces(spread), axis=0), to_patch[...])
    sent = sent[0:96] + sent[96:192] + sent[192:288]
    send[:, 0:128] = meta[...]
    send[:, 128:256] = jnp.concatenate([sent, jnp.zeros((CAP, DEV), F32)], axis=0).T


def pack(to_patch, to_slot, meta, outer, inner, early):
    return pl.pallas_call(
        pack_kernel,
        out_shape=jax.ShapeDtypeStruct((DEV, 256), F32),
        in_specs=[vmem()] * 6,
        out_specs=vmem(),
        compiler_params=params(),
        name="pack",
    )(to_patch, to_slot, meta, outer, inner, early)


def pieces(param):
    other = 1.0 - param
    return [
        other * other * other / 6.0,
        (3.0 * param * param * param - 6.0 * param * param + 4.0) / 6.0,
        (-3.0 * param * param * param + 3.0 * param * param + 3.0 * param + 1.0) / 6.0,
        param * param * param / 6.0,
    ]


def gather_kernel(got, early, inner, outer, field, grads, table, left, right, sems):
    writes = [
        pltpu.make_async_copy(early, field.at[:, 4:28, 8:24], sems.at[0]),
        pltpu.make_async_copy(inner.at[:, :, 0:8], field.at[:, 4:28, 24:32], sems.at[3]),
        pltpu.make_async_copy(inner.at[:, :, 8:16], field.at[:, 4:28, 0:8], sems.at[4]),
        pltpu.make_async_copy(outer.at[:, 0:4], field.at[:, 0:4], sems.at[1]),
        pltpu.make_async_copy(outer.at[:, 4:8], field.at[:, 28:32], sems.at[2]),
    ]
    for write in writes:
        write.start()
    table[0:128] = got[:, 0:128].T
    table[128:256] = got[:, 128:256].T
    basis_u = pieces(table[64:96])
    basis_v = pieces(table[96:128])
    knot = lax.broadcasted_iota(jnp.int32, (NC, DEV), 0).astype(F32)

    def spline(span, basis, slot):
        offset = knot - table[span + slot : span + slot + 1]
        rows = jnp.zeros((NC, DEV), F32)
        for index in range(4):
            rows = jnp.where(offset == float(index), basis[index][slot : slot + 1], rows)
        return rows

    product = jnp.zeros((6 * NC, 2 * NC), F32)
    for slot in range(CAP):
        part = slice(DEV * slot, DEV * slot + DEV)
        along_u = spline(0, basis_u, slot)
        for k in range(3):
            value = table[128 + CAP * k + slot : 128 + CAP * k + slot + 1]
            high, low = two_pieces(along_u * value)
            left[NC * k : NC * k + NC, part] = high
            left[3 * NC + NC * k : 3 * NC + NC * k + NC, part] = low
        high, low = two_pieces(spline(CAP, basis_v, slot))
        right[0:NC, part] = high
        right[NC : 2 * NC, part] = low
        if slot % CHUNK == CHUNK - 1:
            block = slice(DEV * (slot + 1 - CHUNK), DEV * (slot + 1))
            product = product + dot_nt(left[:, block], right[:, block])
    total = product[0 : 3 * NC, 0:NC] + (
        product[0 : 3 * NC, NC : 2 * NC] + product[3 * NC : 6 * NC, 0:NC]
    )
    grads[0] = total.reshape(3, NC, NC)
    for write in writes:
        write.wait()


def gather(got, early, inner, outer):
    return pl.pallas_call(
        gather_kernel,
        out_shape=(
            jax.ShapeDtypeStruct((3, NX, NY, NZ), F32),
            jax.ShapeDtypeStruct((1, 3, NC, NC), F32),
        ),
        in_specs=[vmem()] * 4,
        out_specs=(pl.BlockSpec(memory_space=pl.ANY), vmem()),
        scratch_shapes=[
            pltpu.VMEM((256, DEV), F32),
            pltpu.VMEM((6 * NC, DEV * CAP), BF16),
            pltpu.VMEM((2 * NC, DEV * CAP), BF16),
            pltpu.SemaphoreType.DMA((5,)),
        ],
        compiler_params=params(),
        cost_estimate=pl.CostEstimate(flops=400_000_000, bytes_accessed=200_000, transcendentals=0),
        name="gather",
    )(got, early, inner, outer)


def body(volume_sens, stiffness, patch_of_row, knot_spans, span_params):
    y_one, y_two, x_one, x_two = messages(
        pltpu.with_memory_space_constraint(volume_sens, pltpu.HBM),
        pltpu.with_memory_space_constraint(stiffness, pltpu.HBM),
    )
    ya, yb = exchange(False, y_one, y_two)
    xa, xb = exchange(True, x_one, x_two)
    to_patch, to_slot, meta = route(
        patch_of_row.reshape(1, ROWS), knot_spans[0].T, span_params[0].T
    )
    early, early_surface, planes, cubes = ahead(volume_sens, stiffness)
    za, zb = exchange(True, *corners(ya, yb, meta, early_surface))
    inner, inner_surface, keep, keep3 = interior(volume_sens, stiffness, ya, yb, planes, cubes)
    outer, outer_surface = edges(volume_sens, ya, yb, xa, xb, za, zb, keep, keep3)
    send = pack(to_patch, to_slot, meta, outer_surface, inner_surface, early_surface)
    got = lax.all_to_all(send, ("gx", "gy"), 0, 0, tiled=True)
    return gather(got, early, inner, outer)


def solution(mesh):
    placed = (
        P(None, "gx", "gy", None),
        P("gx", "gy", None),
        P(("gx", "gy"), None, None),
        P(("gx", "gy"), None, None),
        P(("gx", "gy"), None, None),
    )
    return jax.shard_map(
        body,
        mesh=mesh,
        in_specs=placed,
        out_specs=(P(None, "gx", "gy", None), P(("gx", "gy"), None, None, None)),
        check_vma=False,
    )
```

```python
import jax
import jax.numpy as jnp
from jax import lax
from jax.experimental import pallas as pl
from jax.experimental.pallas import tpu as pltpu
from jax.sharding import PartitionSpec as P

NC = 64
OMEGA = 2.0 / 3.0
KEEP = 1.0 - OMEGA
NX = 32
NY = 32
NZ = 128
ROWS = NX * NY
CAP = 32
DEV = 128
CHUNK = 8
EX = NX + 8
EY = NY + 8
SLAB_V = 9 * NX
SLAB = 13 * NX
F32 = jnp.float32
BF16 = jnp.bfloat16
VMEM_LIMIT = 24 * 1024 * 1024


def vmem():
    return pl.BlockSpec(memory_space=pltpu.VMEM)


def params():
    return pltpu.CompilerParams(vmem_limit_bytes=VMEM_LIMIT)


def is_even(axis):
    return lax.rem(lax.axis_index(axis), 2) == 0


def exchange(along_x, one, two):
    count_x, count_y = lax.axis_size("gx"), lax.axis_size("gy")

    def partner(i, last):
        return i if i in (0, last) else ((i + 1) ^ 1) - 1

    first, second = [], []
    for i in range(count_x):
        for j in range(count_y):
            if along_x:
                near, far = (i ^ 1, j), (partner(i, count_x - 1), j)
                far = (count_x - 1 - i, j) if far == (i, j) else far
            else:
                near, far = (i, j ^ 1), (i, partner(j, count_y - 1))
                far = (i ^ 1, j) if far == (i, j) else far
            here = i * count_y + j
            first.append((here, near[0] * count_y + near[1]))
            second.append((here, far[0] * count_y + far[1]))
    both = ("gx", "gy")
    far = lax.ppermute(two, both, second)
    return lax.ppermute(one, both, first), far


def at_end(axis):
    here = lax.axis_index(axis)
    return jnp.logical_or(here == 0, here == lax.axis_size(axis) - 1)


def two_pieces(x):
    high = x.astype(BF16)
    return high, (x - high.astype(F32)).astype(BF16)


def three_pieces(x):
    high = x.astype(BF16)
    rest = x - high.astype(F32)
    mid = rest.astype(BF16)
    return high, mid, (rest - mid.astype(F32)).astype(BF16)


def dot(a, b):
    return jnp.dot(a, b, preferred_element_type=F32)


def dot_nt(a, b):
    return lax.dot_general(a, b, (((1,), (1,)), ((), ())), preferred_element_type=F32)


def message_kernel(vs, c, y_one, y_two, x_one, x_two, low_v, high_v, low_c, high_c, sems):
    slabs = [
        pltpu.make_async_copy(vs.at[:, :, 0:8], low_v, sems.at[0]),
        pltpu.make_async_copy(vs.at[:, :, NY - 8 : NY], high_v, sems.at[1]),
        pltpu.make_async_copy(c.at[:, 0:8], low_c, sems.at[2]),
        pltpu.make_async_copy(c.at[:, NY - 8 : NY], high_c, sems.at[3]),
    ]
    for copy in slabs:
        copy.start()

    def layers(low, high):
        copies = []
        for k in range(3):
            spot = slice(3 * k, 3 * k + 3)
            copies.append(pltpu.make_async_copy(vs.at[k, 0:3], low.at[spot], sems.at[4 + k]))
            copies.append(
                pltpu.make_async_copy(vs.at[k, NX - 3 : NX], high.at[spot], sems.at[7 + k])
            )
        copies.append(pltpu.make_async_copy(c.at[0:4], low.at[9:13], sems.at[10]))
        copies.append(pltpu.make_async_copy(c.at[NX - 4 : NX], high.at[9:13], sems.at[11]))
        return copies

    even_x = is_even("gx")
    even_y = is_even("gy")

    @pl.when(even_x)
    def _():
        for copy in layers(x_two, x_one):
            copy.start()

    @pl.when(jnp.logical_not(even_x))
    def _():
        for copy in layers(x_one, x_two):
            copy.start()

    inside_y = jnp.where(at_end("gy"), 0.0, 1.0)

    def put(row, size, low, high):
        y_one[row : row + size] = jnp.where(even_y, high, low)
        y_two[row : row + size] = jnp.where(even_y, low, high) * inside_y

    for copy in slabs:
        copy.wait()
    for x in range(NX):
        for k in range(3):
            put(9 * x + 3 * k, 3, low_v[k, x, 0:3], high_v[k, x, 5:8])
        put(SLAB_V + 4 * x, 4, low_c[x, 0:4], high_c[x, 4:8])

    @pl.when(even_x)
    def _():
        for copy in layers(x_two, x_one):
            copy.wait()

    @pl.when(jnp.logical_not(even_x))
    def _():
        for copy in layers(x_one, x_two):
            copy.wait()

    @pl.when(at_end("gx"))
    def _():
        x_two[...] = jnp.zeros((13, NY, NZ), F32)


def messages(vs, c):
    y_shape = jax.ShapeDtypeStruct((SLAB, NZ), F32)
    x_shape = jax.ShapeDtypeStruct((13, NY, NZ), F32)
    return pl.pallas_call(
        message_kernel,
        out_shape=(y_shape, y_shape, x_shape, x_shape),
        in_specs=[pl.BlockSpec(memory_space=pltpu.HBM)] * 2,
        out_specs=(vmem(),) * 4,
        scratch_shapes=[
            pltpu.VMEM((3, NX, 8, NZ), F32),
            pltpu.VMEM((3, NX, 8, NZ), F32),
            pltpu.VMEM((NX, 8, NZ), F32),
            pltpu.VMEM((NX, 8, NZ), F32),
            pltpu.SemaphoreType.DMA((12,)),
        ],
        compiler_params=params(),
        name="messages",
    )(vs, c)


def y_halo(even, one, two, first, size, before):
    rows = slice(first, first + size)
    return jnp.where(even == before, two[rows], one[rows])


def corner_kernel(yb, ya, _, __, one, two):
    even_x = is_even("gx")
    even_y = is_even("gy")
    inside_x = jnp.where(at_end("gx"), 0.0, 1.0)
    blank = jnp.zeros((2, NZ), F32)
    for i in range(13):
        if i < 9:
            k, layer = divmod(i, 3)
            size, places = 3, (9 * layer + 3 * k, 9 * (NX - 3 + layer) + 3 * k)
            one[i, 3:5] = blank
            two[i, 3:5] = blank
        else:
            size, places = 4, (SLAB_V + 4 * (i - 9), SLAB_V + 4 * (NX - 4 + i - 9))
        for spot, before in ((slice(0, size), False), (slice(8 - size, 8), True)):
            low, high = (y_halo(even_y, ya, yb, row, size, before) for row in places)
            one[i, spot] = jnp.where(even_x, high, low)
            two[i, spot] = jnp.where(even_x, low, high) * inside_x


def corners(ya, yb, meta, early):
    shape = jax.ShapeDtypeStruct((13, 8, NZ), F32)
    return pl.pallas_call(
        corner_kernel,
        out_shape=(shape, shape),
        in_specs=[vmem()] * 4,
        out_specs=(vmem(), vmem()),
        compiler_params=params(),
        name="corners",
    )(yb, ya, meta, early)


def route_kernel(patch, spans, par, to_patch, to_slot, meta):
    patch_row = patch[...]
    hot = (lax.broadcasted_iota(jnp.int32, (DEV, ROWS), 0) == patch_row).astype(F32)
    hot16 = hot.astype(BF16)
    to_patch[...] = hot16
    upper = (
        lax.broadcasted_iota(jnp.int32, (128, 128), 0)
        <= lax.broadcasted_iota(jnp.int32, (128, 128), 1)
    ).astype(BF16)
    before = jnp.zeros((DEV, 1), F32)
    ranks = []
    for block in range(ROWS // 128):
        part = slice(128 * block, 128 * block + 128)
        count = dot(hot16[:, part], upper) + before
        ranks.append(jnp.sum(count * hot[:, part], axis=0, keepdims=True) - 1.0)
        before = count[:, 127:128]
    rank = jnp.concatenate(ranks, axis=1)
    slot_hot = (lax.broadcasted_iota(jnp.int32, (CAP, ROWS), 0).astype(F32) == rank).astype(F32)
    to_slot[...] = slot_hot
    fields = [
        spans[0:1].astype(F32),
        spans[1:2].astype(F32),
        par[0:1],
        par[1:2],
    ]
    spread = jnp.concatenate(
        [slot_hot * field for field in fields], axis=0
    )
    high, mid, low = three_pieces(spread)
    meta[...] = dot_nt(hot16, high) + dot_nt(hot16, mid) + dot_nt(hot16, low)


def route(patch, spans, par):
    return pl.pallas_call(
        route_kernel,
        out_shape=(
            jax.ShapeDtypeStruct((DEV, ROWS), BF16),
            jax.ShapeDtypeStruct((CAP, ROWS), F32),
            jax.ShapeDtypeStruct((DEV, 128), F32),
        ),
        in_specs=[vmem()] * 3,
        out_specs=(vmem(),) * 3,
        compiler_params=params(),
        cost_estimate=pl.CostEstimate(flops=400_000_000, bytes_accessed=2_000_000, transcendentals=0),
        name="route",
    )(patch, spans, par)


def up(x):
    return pltpu.roll(x, x.shape[0] - 1, 0)


def down(x):
    return pltpu.roll(x, 1, 0)


class Rows:
    def __init__(self):
        self.place = {}

    def hold(self, ref, rows):
        for index, x in enumerate(rows):
            self.place[x] = (ref, index)
        return self

    def __getitem__(self, x):
        ref, index = self.place[x]
        return ref[index]

    def __setitem__(self, x, value):
        ref, index = self.place[x]
        ref[index] = value


EDGE = [4, 5, 6, 7, 8, 31, 32, 33, 34, 35]
MIDDLE = list(range(9, 31))


class Joined:
    def __init__(self, whole, rest, ahead):
        self.whole, self.rest, self.ahead = whole, rest, ahead

    def __getitem__(self, x):
        if x in EDGE:
            return self.whole[EDGE.index(x)]
        spot = MIDDLE.index(x)
        return jnp.concatenate(
            [self.rest[spot, 16:24], self.ahead[x - 5, 8:24], self.rest[spot, 0:16]], axis=0
        )

    def __setitem__(self, x, value):
        if x in EDGE:
            spot = EDGE.index(x)
            self.whole[spot, 24:40] = value[0:16]
            self.whole[spot, 8:24] = self.ahead[x - 5, 8:24]
            self.whole[spot, 0:8] = value[16:24]
        else:
            self.rest[MIDDLE.index(x)] = value


def all_rows(v):
    return v


def outer_rows(v):
    return jnp.concatenate([v[24:40], v[0:8]], axis=0)


def last_outer_rows(v):
    return jnp.concatenate([v[24:32], v[0:8]], axis=0)


def inner_rows(v):
    return v[8:24]


def center_rows(v):
    return v[0:NY]


class Stencil:
    def __init__(self, part, last_part, height, stiff, ratio, wx, wy, wz, scale, y0, y1, y2):
        self.part, self.last_part = part, last_part
        self.stiff, self.ratio, self.scale = stiff, ratio, scale
        self.wx, self.wy, self.wz = wx, wy, wz
        self.fields = (y0, y1, y2)
        lane = lax.broadcasted_iota(jnp.int32, (height, NZ), 1)
        self.not_last = lane < NZ - 1
        self.not_first = lane > 0

    def prepare(self, x, source):
        part = self.part
        whole = self.stiff[x]
        here, after, before = part(whole), part(self.stiff[x + 1]), part(self.stiff[x - 1])
        y_next = part(up(whole))
        z_next = jnp.where(self.not_last, pltpu.roll(here, NZ - 1, 1), 0.0)
        z_prev = jnp.where(self.not_first, pltpu.roll(here, 1, 1), 0.0)
        sides = (before + after) + (y_next + part(down(whole))) + (z_next + z_prev)
        diag = 3.0 * here + 0.5 * sides
        inverse = jnp.where(here > 0.0, 1.0 / diag, 0.0)
        self.ratio[x] = OMEGA * inverse
        self.wx[x] = 0.5 * (here + after)
        self.wy[x] = 0.5 * (here + y_next)
        self.wz[x] = jnp.where(self.not_last, 0.5 * (here + z_next), 0.0)
        self.scale[x] = diag
        for k in range(3):
            self.fields[0][k][x] = source(k, x) * inverse

    def update(self, level, k, x, part):
        source = self.fields[level][k]
        whole, face_y = source[x], self.wy[x]
        here, face_z = part(whole), part(self.wz[x])
        total = part(self.wx[x]) * part(source[x + 1]) + part(self.wx[x - 1]) * part(source[x - 1])
        total = total + (part(face_y) * part(up(whole)) + part(down(face_y * whole)))
        total = total + (
            face_z * pltpu.roll(here, NZ - 1, 1) + pltpu.roll(face_z * here, 1, 1)
        )
        return part(self.fields[0][k][x]) + KEEP * here + part(self.ratio[x]) * total

    def sweep(self, level, rows):
        for x in rows:
            for k in range(3):
                self.fields[level + 1][k][x] = self.update(level, k, x, self.part)

    def finish(self, x, out, surface, index):
        for k in range(3):
            fresh = self.update(2, k, x, self.last_part)
            surface[k, index] = fresh
            out[k, index] = fresh * self.last_part(self.scale[x])


PREPARED = list(range(5, 35))


def ahead_kernel(vs, c, out, surface, planes, cubes):
    class Given:
        def __getitem__(self, x):
            return c[x - 4]

    fields = [[Rows().hold(cubes.at[n, k], PREPARED) for k in range(3)] for n in range(3)]
    grid = Stencil(
        all_rows, inner_rows, NY, Given(),
        *(Rows().hold(planes.at[n], PREPARED) for n in range(5)), *fields,
    )
    for x in range(5, 35):
        grid.prepare(x, lambda k, x: vs[k, x - 4])
    grid.sweep(0, range(6, 34))
    grid.sweep(1, range(7, 33))
    for x in range(8, 32):
        grid.finish(x, out, surface, x - 8)


def ahead(vs, c):
    rows = jax.ShapeDtypeStruct((3, 24, 16, NZ), F32)
    return pl.pallas_call(
        ahead_kernel,
        out_shape=(
            rows,
            rows,
            jax.ShapeDtypeStruct((5, len(PREPARED), NY, NZ), F32),
            jax.ShapeDtypeStruct((3, 3, len(PREPARED), NY, NZ), F32),
        ),
        in_specs=[vmem()] * 2,
        out_specs=(vmem(),) * 4,
        compiler_params=params(),
        cost_estimate=pl.CostEstimate(flops=60_000_000, bytes_accessed=6_000_000, transcendentals=0),
        name="ahead",
    )(vs, c)


def interior_kernel(
    vs, c, yb, ya, planes, cubes, out, surface, keep, keep3, stiff, rest, rest3, halo,
):
    even_y = is_even("gy")
    for x in range(NX):
        row = SLAB_V + 4 * x
        stiff[x, 0:NY] = c[x]
        stiff[x, NY : NY + 4] = y_halo(even_y, ya, yb, row, 4, False)
        stiff[x, EY - 4 : EY] = y_halo(even_y, ya, yb, row, 4, True)
    for x in range(1, NX - 1):
        for k in range(3):
            row = 9 * x + 3 * k
            halo[k, x, 0:3] = y_halo(even_y, ya, yb, row, 3, False)
            halo[k, x, 5:8] = y_halo(even_y, ya, yb, row, 3, True)

    def source(k, x):
        return jnp.concatenate([vs[k, x - 4, 24:32], halo[k, x - 4], vs[k, x - 4, 0:8]], axis=0)

    fields = [
        [Joined(keep3.at[n, k], rest3.at[n, k], cubes.at[n, k]) for k in range(3)] for n in range(3)
    ]
    grid = Stencil(
        outer_rows, last_outer_rows, 24, Rows().hold(stiff, range(4, 36)),
        *(Joined(keep.at[n], rest.at[n], planes.at[n]) for n in range(5)), *fields,
    )
    for x in (4, 5, 34, 35):
        keep[5, EDGE.index(x)] = grid.stiff[x]
    for x in range(5, 35):
        grid.prepare(x, source)
    grid.sweep(0, range(6, 34))
    grid.sweep(1, range(7, 33))
    for x in range(8, 32):
        grid.finish(x, out, surface, x - 8)


def interior(vs, c, ya, yb, planes, cubes):
    rows = jax.ShapeDtypeStruct((3, 24, 16, NZ), F32)
    return pl.pallas_call(
        interior_kernel,
        out_shape=(
            rows,
            rows,
            jax.ShapeDtypeStruct((6, len(EDGE), EY, NZ), F32),
            jax.ShapeDtypeStruct((3, 3, len(EDGE), EY, NZ), F32),
        ),
        in_specs=[vmem()] * 6,
        out_specs=(vmem(),) * 4,
        scratch_shapes=[
            pltpu.VMEM((NX, EY, NZ), F32),
            pltpu.VMEM((5, len(MIDDLE), 24, NZ), F32),
            pltpu.VMEM((3, 3, len(MIDDLE), 24, NZ), F32),
            pltpu.VMEM((3, NX, 8, NZ), F32),
        ],
        compiler_params=params(),
        cost_estimate=pl.CostEstimate(flops=60_000_000, bytes_accessed=6_000_000, transcendentals=0),
        name="interior",
    )(vs, c, yb, ya, planes, cubes)


def edge_kernel(
    vs, yb, ya, xb, xa, zb, za, keep, keep3, out, surface, fresh, fresh3,
):
    even_x = is_even("gx")
    even_y = is_even("gy")

    def x_halo(layer, before):
        center = jnp.where(even_x == before, xb[layer], xa[layer])
        corner = jnp.where(even_x == before, zb[layer], za[layer])
        return jnp.concatenate([center, corner], axis=0)

    class Given:
        def __getitem__(self, x):
            if x < 4:
                return x_halo(9 + x, True)
            if x < 36:
                return keep[5, EDGE.index(x)]
            return x_halo(9 + x - 36, False)

    def source(k, x):
        if x == 4 or x == 35:
            spot = 0 if x == 4 else 1
            row = 9 * (x - 4) + 3 * k
            fresh3[3, k, spot, NY : NY + 3] = y_halo(even_y, ya, yb, row, 3, False)
            fresh3[3, k, spot, EY - 3 : EY] = y_halo(even_y, ya, yb, row, 3, True)
            return jnp.concatenate([vs[k, x - 4], fresh3[3, k, spot, NY:EY]], axis=0)
        if x < 4:
            return x_halo(3 * k + x - 1, True)
        return x_halo(3 * k + x - 36, False)

    def hold(ref3, n, k, rows):
        return Rows().hold(keep3.at[n, k], EDGE).hold(ref3.at[n, k], rows)

    first = [1, 2, 3, 4, 35, 36, 37, 38]
    second = [2, 3, 4, 5, 34, 35, 36, 37]
    third = [3, 4, 5, 6, 33, 34, 35, 36]
    last = [4, 5, 6, 7, 32, 33, 34, 35]
    planes = [Rows().hold(keep.at[n], EDGE).hold(fresh.at[n], first) for n in range(5)]
    fields = [
        [hold(fresh3, n, k, rows) for k in range(3)] for n, rows in enumerate((first, second, third))
    ]
    grid = Stencil(all_rows, center_rows, EY, Given(), *planes, *fields)
    for x in first:
        grid.prepare(x, source)
    grid.sweep(0, second)
    grid.sweep(1, third)
    for index, x in enumerate(last):
        grid.finish(x, out, surface, index)


def edges(vs, ya, yb, xa, xb, za, zb, keep, keep3):
    rows = jax.ShapeDtypeStruct((3, 8, NY, NZ), F32)
    return pl.pallas_call(
        edge_kernel,
        out_shape=(rows, rows),
        in_specs=[vmem()] * 9,
        out_specs=(vmem(),) * 2,
        scratch_shapes=[
            pltpu.VMEM((5, 8, EY, NZ), F32),
            pltpu.VMEM((4, 3, 8, EY, NZ), F32),
        ],
        compiler_params=params(),
        cost_estimate=pl.CostEstimate(flops=20_000_000, bytes_accessed=2_000_000, transcendentals=0),
        name="edges",
    )(vs, yb, ya, xb, xa, zb, za, keep, keep3)


def pack_kernel(to_patch, to_slot, meta, outer, inner, early, send):
    column = lax.broadcasted_iota(jnp.int32, (DEV, NZ), 1)
    values = []
    for block in range(ROWS // DEV):
        pieces_of = [[], [], []]
        for k in range(3):
            for x in range(4 * block, 4 * block + 4):
                if 4 <= x < 28:
                    pieces_of[k] += [inner[k, x - 4, 8:16], early[k, x - 4], inner[k, x - 4, 0:8]]
                else:
                    pieces_of[k].append(outer[k, x if x < 4 else x - 24])
        first, second, third = (jnp.concatenate(p, axis=0) for p in pieces_of)
        mixed = jnp.where(column == 1, pltpu.roll(second, 1, 1), first)
        mixed = jnp.where(column == 2, pltpu.roll(third, 2, 1), mixed)
        values.append(OMEGA * mixed.T[0:3])
    values = jnp.concatenate(values, axis=1)
    slots = to_slot[...]
    spread = jnp.concatenate([slots * values[k : k + 1] for k in range(3)], axis=0)
    sent = dot_nt(jnp.concatenate(three_pieces(spread), axis=0), to_patch[...])
    sent = sent[0:96] + sent[96:192] + sent[192:288]
    send[:, 0:128] = meta[...]
    send[:, 128:256] = jnp.concatenate([sent, jnp.zeros((CAP, DEV), F32)], axis=0).T


def pack(to_patch, to_slot, meta, outer, inner, early):
    return pl.pallas_call(
        pack_kernel,
        out_shape=jax.ShapeDtypeStruct((DEV, 256), F32),
        in_specs=[vmem()] * 6,
        out_specs=vmem(),
        compiler_params=params(),
        name="pack",
    )(to_patch, to_slot, meta, outer, inner, early)


def pieces(param):
    other = 1.0 - param
    return [
        other * other * other / 6.0,
        (3.0 * param * param * param - 6.0 * param * param + 4.0) / 6.0,
        (-3.0 * param * param * param + 3.0 * param * param + 3.0 * param + 1.0) / 6.0,
        param * param * param / 6.0,
    ]


def gather_kernel(got, early, inner, outer, field, grads, table, left, right, sems):
    writes = [
        pltpu.make_async_copy(early, field.at[:, 4:28, 8:24], sems.at[0]),
        pltpu.make_async_copy(inner.at[:, :, 0:8], field.at[:, 4:28, 24:32], sems.at[3]),
        pltpu.make_async_copy(inner.at[:, :, 8:16], field.at[:, 4:28, 0:8], sems.at[4]),
        pltpu.make_async_copy(outer.at[:, 0:4], field.at[:, 0:4], sems.at[1]),
        pltpu.make_async_copy(outer.at[:, 4:8], field.at[:, 28:32], sems.at[2]),
    ]
    for write in writes:
        write.start()
    table[0:128] = got[:, 0:128].T
    table[128:256] = got[:, 128:256].T
    basis_u = pieces(table[64:96])
    basis_v = pieces(table[96:128])
    knot = lax.broadcasted_iota(jnp.int32, (NC, DEV), 0).astype(F32)

    def spline(span, basis, slot):
        offset = knot - table[span + slot : span + slot + 1]
        rows = jnp.zeros((NC, DEV), F32)
        for index in range(4):
            rows = jnp.where(offset == float(index), basis[index][slot : slot + 1], rows)
        return rows

    product = jnp.zeros((6 * NC, 2 * NC), F32)
    for slot in range(CAP):
        part = slice(DEV * slot, DEV * slot + DEV)
        along_u = spline(0, basis_u, slot)
        for k in range(3):
            value = table[128 + CAP * k + slot : 128 + CAP * k + slot + 1]
            high, low = two_pieces(along_u * value)
            left[NC * k : NC * k + NC, part] = high
            left[3 * NC + NC * k : 3 * NC + NC * k + NC, part] = low
        high, low = two_pieces(spline(CAP, basis_v, slot))
        right[0:NC, part] = high
        right[NC : 2 * NC, part] = low
        if slot % CHUNK == CHUNK - 1:
            block = slice(DEV * (slot + 1 - CHUNK), DEV * (slot + 1))
            product = product + dot_nt(left[:, block], right[:, block])
    total = product[0 : 3 * NC, 0:NC] + (
        product[0 : 3 * NC, NC : 2 * NC] + product[3 * NC : 6 * NC, 0:NC]
    )
    grads[0] = total.reshape(3, NC, NC)
    for write in writes:
        write.wait()


def gather(got, early, inner, outer):
    return pl.pallas_call(
        gather_kernel,
        out_shape=(
            jax.ShapeDtypeStruct((3, NX, NY, NZ), F32),
            jax.ShapeDtypeStruct((1, 3, NC, NC), F32),
        ),
        in_specs=[vmem()] * 4,
        out_specs=(pl.BlockSpec(memory_space=pl.ANY), vmem()),
        scratch_shapes=[
            pltpu.VMEM((256, DEV), F32),
            pltpu.VMEM((6 * NC, DEV * CAP), BF16),
            pltpu.VMEM((2 * NC, DEV * CAP), BF16),
            pltpu.SemaphoreType.DMA((5,)),
        ],
        compiler_params=params(),
        cost_estimate=pl.CostEstimate(flops=400_000_000, bytes_accessed=200_000, transcendentals=0),
        name="gather",
    )(got, early, inner, outer)


def body(volume_sens, stiffness, patch_of_row, knot_spans, span_params):
    y_one, y_two, x_one, x_two = messages(
        pltpu.with_memory_space_constraint(volume_sens, pltpu.HBM),
        pltpu.with_memory_space_constraint(stiffness, pltpu.HBM),
    )
    ya, yb = exchange(False, y_one, y_two)
    xa, xb = exchange(True, x_one, x_two)
    to_patch, to_slot, meta = route(
        patch_of_row.reshape(1, ROWS), knot_spans[0].T, span_params[0].T
    )
    early, early_surface, planes, cubes = ahead(volume_sens, stiffness)
    za, zb = exchange(True, *corners(ya, yb, meta, early_surface))
    inner, inner_surface, keep, keep3 = interior(volume_sens, stiffness, ya, yb, planes, cubes)
    outer, outer_surface = edges(volume_sens, ya, yb, xa, xb, za, zb, keep, keep3)
    send = pack(to_patch, to_slot, meta, outer_surface, inner_surface, early_surface)
    got = lax.all_to_all(send, ("gx", "gy"), 0, 0, tiled=True)
    return gather(got, early, inner, outer)


def solution(mesh):
    placed = (
        P(None, "gx", "gy", None),
        P("gx", "gy", None),
        P(("gx", "gy"), None, None),
        P(("gx", "gy"), None, None),
        P(("gx", "gy"), None, None),
    )
    return jax.shard_map(
        body,
        mesh=mesh,
        in_specs=placed,
        out_specs=(P(None, "gx", "gy", None), P(("gx", "gy"), None, None, None)),
        check_vma=False,
    )
```

```python
import jax
import jax.numpy as jnp
from jax import lax
from jax.experimental import pallas as pl
from jax.experimental.pallas import tpu as pltpu
from jax.sharding import PartitionSpec as P

NC = 64
OMEGA = 2.0 / 3.0
KEEP = 1.0 - OMEGA
NX = 32
NY = 32
NZ = 128
ROWS = NX * NY
CAP = 32
DEV = 128
CHUNK = 8
EX = NX + 8
EY = NY + 8
SLAB_V = 9 * NX
SLAB = 13 * NX
F32 = jnp.float32
BF16 = jnp.bfloat16
VMEM_LIMIT = 24 * 1024 * 1024


def vmem():
    return pl.BlockSpec(memory_space=pltpu.VMEM)


def params():
    return pltpu.CompilerParams(vmem_limit_bytes=VMEM_LIMIT)


def is_even(axis):
    return lax.rem(lax.axis_index(axis), 2) == 0


def exchange(along_x, one, two):
    count_x, count_y = lax.axis_size("gx"), lax.axis_size("gy")

    def partner(i, last):
        return i if i in (0, last) else ((i + 1) ^ 1) - 1

    first, second = [], []
    for i in range(count_x):
        for j in range(count_y):
            if along_x:
                near, far = (i ^ 1, j), (partner(i, count_x - 1), j)
                far = (count_x - 1 - i, j) if far == (i, j) else far
            else:
                near, far = (i, j ^ 1), (i, partner(j, count_y - 1))
                far = (i ^ 1, j) if far == (i, j) else far
            here = i * count_y + j
            first.append((here, near[0] * count_y + near[1]))
            second.append((here, far[0] * count_y + far[1]))
    both = ("gx", "gy")
    far = lax.ppermute(two, both, second)
    return lax.ppermute(one, both, first), far


def at_end(axis):
    here = lax.axis_index(axis)
    return jnp.logical_or(here == 0, here == lax.axis_size(axis) - 1)


def two_pieces(x):
    high = x.astype(BF16)
    return high, (x - high.astype(F32)).astype(BF16)


def three_pieces(x):
    high = x.astype(BF16)
    rest = x - high.astype(F32)
    mid = rest.astype(BF16)
    return high, mid, (rest - mid.astype(F32)).astype(BF16)


def dot(a, b):
    return jnp.dot(a, b, preferred_element_type=F32)


def dot_nt(a, b):
    return lax.dot_general(a, b, (((1,), (1,)), ((), ())), preferred_element_type=F32)


def message_kernel(vs, c, y_one, y_two, x_one, x_two, low_v, high_v, low_c, high_c, sems):
    slabs = [
        pltpu.make_async_copy(vs.at[:, :, 0:8], low_v, sems.at[0]),
        pltpu.make_async_copy(vs.at[:, :, NY - 8 : NY], high_v, sems.at[1]),
        pltpu.make_async_copy(c.at[:, 0:8], low_c, sems.at[2]),
        pltpu.make_async_copy(c.at[:, NY - 8 : NY], high_c, sems.at[3]),
    ]
    for copy in slabs:
        copy.start()

    def layers(low, high):
        copies = []
        for k in range(3):
            spot = slice(3 * k, 3 * k + 3)
            copies.append(pltpu.make_async_copy(vs.at[k, 0:3], low.at[spot], sems.at[4 + k]))
            copies.append(
                pltpu.make_async_copy(vs.at[k, NX - 3 : NX], high.at[spot], sems.at[7 + k])
            )
        copies.append(pltpu.make_async_copy(c.at[0:4], low.at[9:13], sems.at[10]))
        copies.append(pltpu.make_async_copy(c.at[NX - 4 : NX], high.at[9:13], sems.at[11]))
        return copies

    even_x = is_even("gx")
    even_y = is_even("gy")

    @pl.when(even_x)
    def _():
        for copy in layers(x_two, x_one):
            copy.start()

    @pl.when(jnp.logical_not(even_x))
    def _():
        for copy in layers(x_one, x_two):
            copy.start()

    inside_y = jnp.where(at_end("gy"), 0.0, 1.0)

    def put(row, size, low, high):
        y_one[row : row + size] = jnp.where(even_y, high, low)
        y_two[row : row + size] = jnp.where(even_y, low, high) * inside_y

    for copy in slabs:
        copy.wait()
    for x in range(NX):
        for k in range(3):
            put(9 * x + 3 * k, 3, low_v[k, x, 0:3], high_v[k, x, 5:8])
        put(SLAB_V + 4 * x, 4, low_c[x, 0:4], high_c[x, 4:8])

    @pl.when(even_x)
    def _():
        for copy in layers(x_two, x_one):
            copy.wait()

    @pl.when(jnp.logical_not(even_x))
    def _():
        for copy in layers(x_one, x_two):
            copy.wait()

    @pl.when(at_end("gx"))
    def _():
        x_two[...] = jnp.zeros((13, NY, NZ), F32)


def messages(vs, c):
    y_shape = jax.ShapeDtypeStruct((SLAB, NZ), F32)
    x_shape = jax.ShapeDtypeStruct((13, NY, NZ), F32)
    return pl.pallas_call(
        message_kernel,
        out_shape=(y_shape, y_shape, x_shape, x_shape),
        in_specs=[pl.BlockSpec(memory_space=pltpu.HBM)] * 2,
        out_specs=(vmem(),) * 4,
        scratch_shapes=[
            pltpu.VMEM((3, NX, 8, NZ), F32),
            pltpu.VMEM((3, NX, 8, NZ), F32),
            pltpu.VMEM((NX, 8, NZ), F32),
            pltpu.VMEM((NX, 8, NZ), F32),
            pltpu.SemaphoreType.DMA((12,)),
        ],
        compiler_params=params(),
        name="messages",
    )(vs, c)


def y_halo(even, one, two, first, size, before):
    rows = slice(first, first + size)
    return jnp.where(even == before, two[rows], one[rows])


def corner_kernel(yb, ya, _, one, two):
    even_x = is_even("gx")
    even_y = is_even("gy")
    inside_x = jnp.where(at_end("gx"), 0.0, 1.0)
    blank = jnp.zeros((2, NZ), F32)
    for i in range(13):
        if i < 9:
            k, layer = divmod(i, 3)
            size, places = 3, (9 * layer + 3 * k, 9 * (NX - 3 + layer) + 3 * k)
            one[i, 3:5] = blank
            two[i, 3:5] = blank
        else:
            size, places = 4, (SLAB_V + 4 * (i - 9), SLAB_V + 4 * (NX - 4 + i - 9))
        for spot, before in ((slice(0, size), False), (slice(8 - size, 8), True)):
            low, high = (y_halo(even_y, ya, yb, row, size, before) for row in places)
            one[i, spot] = jnp.where(even_x, high, low)
            two[i, spot] = jnp.where(even_x, low, high) * inside_x


def corners(ya, yb, early):
    shape = jax.ShapeDtypeStruct((13, 8, NZ), F32)
    return pl.pallas_call(
        corner_kernel,
        out_shape=(shape, shape),
        in_specs=[vmem()] * 3,
        out_specs=(vmem(), vmem()),
        compiler_params=params(),
        name="corners",
    )(yb, ya, early)


def route_kernel(patch, spans, par, to_patch, to_slot, meta):
    patch_row = patch[...]
    hot = (lax.broadcasted_iota(jnp.int32, (DEV, ROWS), 0) == patch_row).astype(F32)
    hot16 = hot.astype(BF16)
    to_patch[...] = hot16
    upper = (
        lax.broadcasted_iota(jnp.int32, (128, 128), 0)
        <= lax.broadcasted_iota(jnp.int32, (128, 128), 1)
    ).astype(BF16)
    before = jnp.zeros((DEV, 1), F32)
    ranks = []
    for block in range(ROWS // 128):
        part = slice(128 * block, 128 * block + 128)
        count = dot(hot16[:, part], upper) + before
        ranks.append(jnp.sum(count * hot[:, part], axis=0, keepdims=True) - 1.0)
        before = count[:, 127:128]
    rank = jnp.concatenate(ranks, axis=1)
    slot_hot = (lax.broadcasted_iota(jnp.int32, (CAP, ROWS), 0).astype(F32) == rank).astype(F32)
    to_slot[...] = slot_hot
    fields = [
        spans[0:1].astype(F32),
        spans[1:2].astype(F32),
        par[0:1],
        par[1:2],
    ]
    spread = jnp.concatenate(
        [slot_hot * field for field in fields], axis=0
    )
    high, mid, low = three_pieces(spread)
    meta[...] = dot_nt(hot16, high) + dot_nt(hot16, mid) + dot_nt(hot16, low)


def route(patch, spans, par):
    return pl.pallas_call(
        route_kernel,
        out_shape=(
            jax.ShapeDtypeStruct((DEV, ROWS), BF16),
            jax.ShapeDtypeStruct((CAP, ROWS), F32),
            jax.ShapeDtypeStruct((DEV, 128), F32),
        ),
        in_specs=[vmem()] * 3,
        out_specs=(vmem(),) * 3,
        compiler_params=params(),
        cost_estimate=pl.CostEstimate(flops=400_000_000, bytes_accessed=2_000_000, transcendentals=0),
        name="route",
    )(patch, spans, par)


def up(x):
    return pltpu.roll(x, x.shape[0] - 1, 0)


def down(x):
    return pltpu.roll(x, 1, 0)


class Rows:
    def __init__(self):
        self.place = {}

    def hold(self, ref, rows):
        for index, x in enumerate(rows):
            self.place[x] = (ref, index)
        return self

    def __getitem__(self, x):
        ref, index = self.place[x]
        return ref[index]

    def __setitem__(self, x, value):
        ref, index = self.place[x]
        ref[index] = value


EDGE = [4, 5, 6, 7, 8, 31, 32, 33, 34, 35]
MIDDLE = list(range(9, 31))


class Joined:
    def __init__(self, whole, rest, ahead):
        self.whole, self.rest, self.ahead = whole, rest, ahead

    def __getitem__(self, x):
        if x in EDGE:
            return self.whole[EDGE.index(x)]
        spot = MIDDLE.index(x)
        return jnp.concatenate(
            [self.rest[spot, 16:24], self.ahead[x - 5, 8:24], self.rest[spot, 0:16]], axis=0
        )

    def __setitem__(self, x, value):
        if x in EDGE:
            spot = EDGE.index(x)
            self.whole[spot, 24:40] = value[0:16]
            self.whole[spot, 8:24] = self.ahead[x - 5, 8:24]
            self.whole[spot, 0:8] = value[16:24]
        else:
            self.rest[MIDDLE.index(x)] = value


def all_rows(v):
    return v


def outer_rows(v):
    return jnp.concatenate([v[24:40], v[0:8]], axis=0)


def last_outer_rows(v):
    return jnp.concatenate([v[24:32], v[0:8]], axis=0)


def inner_rows(v):
    return v[8:24]


def center_rows(v):
    return v[0:NY]


class Stencil:
    def __init__(self, part, last_part, height, stiff, ratio, wx, wy, wz, scale, y0, y1, y2):
        self.part, self.last_part = part, last_part
        self.stiff, self.ratio, self.scale = stiff, ratio, scale
        self.wx, self.wy, self.wz = wx, wy, wz
        self.fields = (y0, y1, y2)
        lane = lax.broadcasted_iota(jnp.int32, (height, NZ), 1)
        self.not_last = lane < NZ - 1
        self.not_first = lane > 0

    def prepare(self, x, source):
        part = self.part
        whole = self.stiff[x]
        here, after, before = part(whole), part(self.stiff[x + 1]), part(self.stiff[x - 1])
        y_next = part(up(whole))
        z_next = jnp.where(self.not_last, pltpu.roll(here, NZ - 1, 1), 0.0)
        z_prev = jnp.where(self.not_first, pltpu.roll(here, 1, 1), 0.0)
        sides = (before + after) + (y_next + part(down(whole))) + (z_next + z_prev)
        diag = 3.0 * here + 0.5 * sides
        inverse = jnp.where(here > 0.0, 1.0 / diag, 0.0)
        self.ratio[x] = OMEGA * inverse
        self.wx[x] = 0.5 * (here + after)
        self.wy[x] = 0.5 * (here + y_next)
        self.wz[x] = jnp.where(self.not_last, 0.5 * (here + z_next), 0.0)
        self.scale[x] = diag
        for k in range(3):
            self.fields[0][k][x] = source(k, x) * inverse

    def update(self, level, k, x, part):
        source = self.fields[level][k]
        whole, face_y = source[x], self.wy[x]
        here, face_z = part(whole), part(self.wz[x])
        total = part(self.wx[x]) * part(source[x + 1]) + part(self.wx[x - 1]) * part(source[x - 1])
        total = total + (part(face_y) * part(up(whole)) + part(down(face_y * whole)))
        total = total + (
            face_z * pltpu.roll(here, NZ - 1, 1) + pltpu.roll(face_z * here, 1, 1)
        )
        return part(self.fields[0][k][x]) + KEEP * here + part(self.ratio[x]) * total

    def sweep(self, level, rows):
        for x in rows:
            for k in range(3):
                self.fields[level + 1][k][x] = self.update(level, k, x, self.part)

    def finish(self, x, out, surface, index):
        for k in range(3):
            fresh = self.update(2, k, x, self.last_part)
            surface[k, index] = fresh
            out[k, index] = fresh * self.last_part(self.scale[x])


PREPARED = list(range(5, 35))


def ahead_kernel(vs, c, out, surface, planes, cubes):
    class Given:
        def __getitem__(self, x):
            return c[x - 4]

    fields = [[Rows().hold(cubes.at[n, k], PREPARED) for k in range(3)] for n in range(3)]
    grid = Stencil(
        all_rows, inner_rows, NY, Given(),
        *(Rows().hold(planes.at[n], PREPARED) for n in range(5)), *fields,
    )
    for x in range(5, 35):
        grid.prepare(x, lambda k, x: vs[k, x - 4])
    grid.sweep(0, range(6, 34))
    grid.sweep(1, range(7, 33))
    for x in range(8, 32):
        grid.finish(x, out, surface, x - 8)


def ahead(vs, c):
    rows = jax.ShapeDtypeStruct((3, 24, 16, NZ), F32)
    return pl.pallas_call(
        ahead_kernel,
        out_shape=(
            rows,
            rows,
            jax.ShapeDtypeStruct((5, len(PREPARED), NY, NZ), F32),
            jax.ShapeDtypeStruct((3, 3, len(PREPARED), NY, NZ), F32),
        ),
        in_specs=[vmem()] * 2,
        out_specs=(vmem(),) * 4,
        compiler_params=params(),
        cost_estimate=pl.CostEstimate(flops=60_000_000, bytes_accessed=6_000_000, transcendentals=0),
        name="ahead",
    )(vs, c)


def interior_kernel(
    vs, c, yb, ya, planes, cubes, out, surface, keep, keep3, stiff, rest, rest3, halo,
):
    even_y = is_even("gy")
    for x in range(NX):
        row = SLAB_V + 4 * x
        stiff[x, 0:NY] = c[x]
        stiff[x, NY : NY + 4] = y_halo(even_y, ya, yb, row, 4, False)
        stiff[x, EY - 4 : EY] = y_halo(even_y, ya, yb, row, 4, True)
    for x in range(1, NX - 1):
        for k in range(3):
            row = 9 * x + 3 * k
            halo[k, x, 0:3] = y_halo(even_y, ya, yb, row, 3, False)
            halo[k, x, 5:8] = y_halo(even_y, ya, yb, row, 3, True)

    def source(k, x):
        return jnp.concatenate([vs[k, x - 4, 24:32], halo[k, x - 4], vs[k, x - 4, 0:8]], axis=0)

    fields = [
        [Joined(keep3.at[n, k], rest3.at[n, k], cubes.at[n, k]) for k in range(3)] for n in range(3)
    ]
    grid = Stencil(
        outer_rows, last_outer_rows, 24, Rows().hold(stiff, range(4, 36)),
        *(Joined(keep.at[n], rest.at[n], planes.at[n]) for n in range(5)), *fields,
    )
    for x in (4, 5, 34, 35):
        keep[5, EDGE.index(x)] = grid.stiff[x]
    for x in range(5, 35):
        grid.prepare(x, source)
    grid.sweep(0, range(6, 34))
    grid.sweep(1, range(7, 33))
    for x in range(8, 32):
        grid.finish(x, out, surface, x - 8)


def interior(vs, c, ya, yb, planes, cubes):
    rows = jax.ShapeDtypeStruct((3, 24, 16, NZ), F32)
    return pl.pallas_call(
        interior_kernel,
        out_shape=(
            rows,
            rows,
            jax.ShapeDtypeStruct((6, len(EDGE), EY, NZ), F32),
            jax.ShapeDtypeStruct((3, 3, len(EDGE), EY, NZ), F32),
        ),
        in_specs=[vmem()] * 6,
        out_specs=(vmem(),) * 4,
        scratch_shapes=[
            pltpu.VMEM((NX, EY, NZ), F32),
            pltpu.VMEM((5, len(MIDDLE), 24, NZ), F32),
            pltpu.VMEM((3, 3, len(MIDDLE), 24, NZ), F32),
            pltpu.VMEM((3, NX, 8, NZ), F32),
        ],
        compiler_params=params(),
        cost_estimate=pl.CostEstimate(flops=60_000_000, bytes_accessed=6_000_000, transcendentals=0),
        name="interior",
    )(vs, c, yb, ya, planes, cubes)


def edge_kernel(
    vs, yb, ya, xb, xa, zb, za, keep, keep3, out, surface, fresh, fresh3,
):
    even_x = is_even("gx")
    even_y = is_even("gy")

    def x_halo(layer, before):
        center = jnp.where(even_x == before, xb[layer], xa[layer])
        corner = jnp.where(even_x == before, zb[layer], za[layer])
        return jnp.concatenate([center, corner], axis=0)

    class Given:
        def __getitem__(self, x):
            if x < 4:
                return x_halo(9 + x, True)
            if x < 36:
                return keep[5, EDGE.index(x)]
            return x_halo(9 + x - 36, False)

    def source(k, x):
        if x == 4 or x == 35:
            spot = 0 if x == 4 else 1
            row = 9 * (x - 4) + 3 * k
            fresh3[3, k, spot, NY : NY + 3] = y_halo(even_y, ya, yb, row, 3, False)
            fresh3[3, k, spot, EY - 3 : EY] = y_halo(even_y, ya, yb, row, 3, True)
            return jnp.concatenate([vs[k, x - 4], fresh3[3, k, spot, NY:EY]], axis=0)
        if x < 4:
            return x_halo(3 * k + x - 1, True)
        return x_halo(3 * k + x - 36, False)

    def hold(ref3, n, k, rows):
        return Rows().hold(keep3.at[n, k], EDGE).hold(ref3.at[n, k], rows)

    first = [1, 2, 3, 4, 35, 36, 37, 38]
    second = [2, 3, 4, 5, 34, 35, 36, 37]
    third = [3, 4, 5, 6, 33, 34, 35, 36]
    last = [4, 5, 6, 7, 32, 33, 34, 35]
    planes = [Rows().hold(keep.at[n], EDGE).hold(fresh.at[n], first) for n in range(5)]
    fields = [
        [hold(fresh3, n, k, rows) for k in range(3)] for n, rows in enumerate((first, second, third))
    ]
    grid = Stencil(all_rows, center_rows, EY, Given(), *planes, *fields)
    for x in first:
        grid.prepare(x, source)
    grid.sweep(0, second)
    grid.sweep(1, third)
    for index, x in enumerate(last):
        grid.finish(x, out, surface, index)


def edges(vs, ya, yb, xa, xb, za, zb, keep, keep3):
    rows = jax.ShapeDtypeStruct((3, 8, NY, NZ), F32)
    return pl.pallas_call(
        edge_kernel,
        out_shape=(rows, rows),
        in_specs=[vmem()] * 9,
        out_specs=(vmem(),) * 2,
        scratch_shapes=[
            pltpu.VMEM((5, 8, EY, NZ), F32),
            pltpu.VMEM((4, 3, 8, EY, NZ), F32),
        ],
        compiler_params=params(),
        cost_estimate=pl.CostEstimate(flops=20_000_000, bytes_accessed=2_000_000, transcendentals=0),
        name="edges",
    )(vs, yb, ya, xb, xa, zb, za, keep, keep3)


def pack_kernel(to_patch, to_slot, meta, outer, inner, early, send):
    column = lax.broadcasted_iota(jnp.int32, (DEV, NZ), 1)
    values = []
    for block in range(ROWS // DEV):
        pieces_of = [[], [], []]
        for k in range(3):
            for x in range(4 * block, 4 * block + 4):
                if 4 <= x < 28:
                    pieces_of[k] += [inner[k, x - 4, 8:16], early[k, x - 4], inner[k, x - 4, 0:8]]
                else:
                    pieces_of[k].append(outer[k, x if x < 4 else x - 24])
        first, second, third = (jnp.concatenate(p, axis=0) for p in pieces_of)
        mixed = jnp.where(column == 1, pltpu.roll(second, 1, 1), first)
        mixed = jnp.where(column == 2, pltpu.roll(third, 2, 1), mixed)
        values.append(OMEGA * mixed.T[0:3])
    values = jnp.concatenate(values, axis=1)
    slots = to_slot[...]
    spread = jnp.concatenate([slots * values[k : k + 1] for k in range(3)], axis=0)
    sent = dot_nt(jnp.concatenate(three_pieces(spread), axis=0), to_patch[...])
    sent = sent[0:96] + sent[96:192] + sent[192:288]
    send[:, 0:128] = meta[...]
    send[:, 128:256] = jnp.concatenate([sent, jnp.zeros((CAP, DEV), F32)], axis=0).T


def pack(to_patch, to_slot, meta, outer, inner, early):
    return pl.pallas_call(
        pack_kernel,
        out_shape=jax.ShapeDtypeStruct((DEV, 256), F32),
        in_specs=[vmem()] * 6,
        out_specs=vmem(),
        compiler_params=params(),
        name="pack",
    )(to_patch, to_slot, meta, outer, inner, early)


def pieces(param):
    other = 1.0 - param
    return [
        other * other * other / 6.0,
        (3.0 * param * param * param - 6.0 * param * param + 4.0) / 6.0,
        (-3.0 * param * param * param + 3.0 * param * param + 3.0 * param + 1.0) / 6.0,
        param * param * param / 6.0,
    ]


def gather_kernel(got, early, inner, outer, field, grads, table, left, right, sems):
    writes = [
        pltpu.make_async_copy(early, field.at[:, 4:28, 8:24], sems.at[0]),
        pltpu.make_async_copy(inner.at[:, :, 0:8], field.at[:, 4:28, 24:32], sems.at[3]),
        pltpu.make_async_copy(inner.at[:, :, 8:16], field.at[:, 4:28, 0:8], sems.at[4]),
        pltpu.make_async_copy(outer.at[:, 0:4], field.at[:, 0:4], sems.at[1]),
        pltpu.make_async_copy(outer.at[:, 4:8], field.at[:, 28:32], sems.at[2]),
    ]
    for write in writes:
        write.start()
    table[0:128] = got[:, 0:128].T
    table[128:256] = got[:, 128:256].T
    basis_u = pieces(table[64:96])
    basis_v = pieces(table[96:128])
    knot = lax.broadcasted_iota(jnp.int32, (NC, DEV), 0).astype(F32)

    def spline(span, basis, slot):
        offset = knot - table[span + slot : span + slot + 1]
        rows = jnp.zeros((NC, DEV), F32)
        for index in range(4):
            rows = jnp.where(offset == float(index), basis[index][slot : slot + 1], rows)
        return rows

    product = jnp.zeros((6 * NC, 2 * NC), F32)
    for slot in range(CAP):
        part = slice(DEV * slot, DEV * slot + DEV)
        along_u = spline(0, basis_u, slot)
        for k in range(3):
            value = table[128 + CAP * k + slot : 128 + CAP * k + slot + 1]
            high, low = two_pieces(along_u * value)
            left[NC * k : NC * k + NC, part] = high
            left[3 * NC + NC * k : 3 * NC + NC * k + NC, part] = low
        high, low = two_pieces(spline(CAP, basis_v, slot))
        right[0:NC, part] = high
        right[NC : 2 * NC, part] = low
        if slot % CHUNK == CHUNK - 1:
            block = slice(DEV * (slot + 1 - CHUNK), DEV * (slot + 1))
            product = product + dot_nt(left[:, block], right[:, block])
    total = product[0 : 3 * NC, 0:NC] + (
        product[0 : 3 * NC, NC : 2 * NC] + product[3 * NC : 6 * NC, 0:NC]
    )
    grads[0] = total.reshape(3, NC, NC)
    for write in writes:
        write.wait()


def gather(got, early, inner, outer):
    return pl.pallas_call(
        gather_kernel,
        out_shape=(
            jax.ShapeDtypeStruct((3, NX, NY, NZ), F32),
            jax.ShapeDtypeStruct((1, 3, NC, NC), F32),
        ),
        in_specs=[vmem()] * 4,
        out_specs=(pl.BlockSpec(memory_space=pl.ANY), vmem()),
        scratch_shapes=[
            pltpu.VMEM((256, DEV), F32),
            pltpu.VMEM((6 * NC, DEV * CAP), BF16),
            pltpu.VMEM((2 * NC, DEV * CAP), BF16),
            pltpu.SemaphoreType.DMA((5,)),
        ],
        compiler_params=params(),
        cost_estimate=pl.CostEstimate(flops=400_000_000, bytes_accessed=200_000, transcendentals=0),
        name="gather",
    )(got, early, inner, outer)


def body(volume_sens, stiffness, patch_of_row, knot_spans, span_params):
    y_one, y_two, x_one, x_two = messages(
        pltpu.with_memory_space_constraint(volume_sens, pltpu.HBM),
        pltpu.with_memory_space_constraint(stiffness, pltpu.HBM),
    )
    ya, yb = exchange(False, y_one, y_two)
    xa, xb = exchange(True, x_one, x_two)
    to_patch, to_slot, meta = route(
        patch_of_row.reshape(1, ROWS), knot_spans[0].T, span_params[0].T
    )
    early, early_surface, planes, cubes = ahead(volume_sens, stiffness)
    za, zb = exchange(True, *corners(ya, yb, early_surface))
    inner, inner_surface, keep, keep3 = interior(volume_sens, stiffness, ya, yb, planes, cubes)
    outer, outer_surface = edges(volume_sens, ya, yb, xa, xb, za, zb, keep, keep3)
    send = pack(to_patch, to_slot, meta, outer_surface, inner_surface, early_surface)
    got = lax.all_to_all(send, ("gx", "gy"), 0, 0, tiled=True)
    return gather(got, early, inner, outer)


def solution(mesh):
    placed = (
        P(None, "gx", "gy", None),
        P("gx", "gy", None),
        P(("gx", "gy"), None, None),
        P(("gx", "gy"), None, None),
        P(("gx", "gy"), None, None),
    )
    return jax.shard_map(
        body,
        mesh=mesh,
        in_specs=placed,
        out_specs=(P(None, "gx", "gy", None), P(("gx", "gy"), None, None, None)),
        check_vma=False,
    )
```
